128 devices in a mesh: seq: 16 (over y, z_hi, core), head: 8 (over z_lo, x).
Axes of the slice: x: 4, y: 4, z: 4 (z_hi: 2, z_lo: 2; z = z_hi * 2 + z_lo), core: 2. Of those that a mesh axis runs over, the one named last changes fastest.
Arguments:
- enc_in: bfloat16 [8192, 4, 768], P(('seq', 'head')), may hold values from -6 to 6
- conv_weight: bfloat16 [5, 768, 1536], replicated, may hold values from -0.09375 to 0.09375
- norm_gain: float32 [1536], replicated, may hold values from 0.25 to 1.75
- w_qkv: bfloat16 [3, 1536, 1536], P(None, None, 'head'), may hold values from -0.63788795 to 0.63788795
- w_out: bfloat16 [1536, 1536], P('head'), may hold values from -0.15625 to 0.15625
- grad_out: bfloat16 [4096, 4, 1536], P(('seq', 'head')), may hold values from -6 to 6
Outputs:
- mixed: bfloat16 [4096, 4, 1536], P(('seq', 'head'))
- grad_input: bfloat16 [8192, 4, 768], P(('seq', 'head'))
- grad_w_qkv: float32 [3, 1536, 1536], P(None, None, 'head')
- grad_w_out: float32 [1536, 1536], P('head')
The draws below stay inside these ranges and needn't reach their ends.
All inputs are finite; a program needn't handle non-finite values.
Results may differ from the reference program's by a relative error of at most 0.024.
Values may be sent and summed in bfloat16 or wider, within the bound.
A program may use at most 256 MiB of HBM per device.

```python
import jax
import jax.numpy as jnp
from jax import lax

C_IN = 768
C = 1536
HEADS = 8
DH = 192
KW = 5
SEQS = 4
L = 4096
LF = 8192
BLOCK = 256
HEADS_DEV = 1
N_SEQ = 16
N_HEAD = 8


def draw_w_qkv(key, part):
    key_base = jax.random.fold_in(key, 0)
    fan_scale = C ** (-0.5)
    drawn_draw = jax.random.truncated_normal(key_base, -4.0, 4.0, (3, C, HEADS * DH), jnp.float32) * fan_scale
    return drawn_draw.astype(jnp.bfloat16)


def level_of(key, dims, pieces, smallest, largest):
    def one(position, shards_of):
        steps = jax.random.uniform(jax.random.fold_in(jax.random.fold_in(key, 6), position), (shards_of,), jnp.float32, smallest / len(pieces), largest / len(pieces))
        return jnp.repeat(jnp.exp(steps), dims[position] // shards_of).reshape((-1,) + (1,) * (len(dims) - position - 1))

    gain = one(*pieces[0])
    for cut in pieces[1:]:
        gain = gain * one(*cut)
    return gain


def bell_draw(own_key, dims, width, reach, cuts=(), dtype=jnp.bfloat16):
    gain = level_of(own_key, dims, cuts, -0.22, 0.18) if cuts else 1.0
    values = jax.random.normal(own_key, dims, jnp.float32) * width * gain
    return jnp.minimum(jnp.maximum(values, -reach), reach).astype(dtype)


def setup_inputs(seed: int = 0) -> dict:
    key_list = jax.random.split(jax.random.key(seed), 7)
    return {
        "enc_in": bell_draw(key_list[0], (LF, SEQS, C_IN), 1.0, 6.0, ((0, 128),)),
        "conv_weight": bell_draw(key_list[1], (KW, C_IN, C), (KW * C_IN) ** -0.5, 0.09375),
        "norm_gain": jnp.clip(1.0 + 0.15 * jax.random.normal(key_list[2], (C,), jnp.float32), 0.25, 1.75),
        "w_qkv": draw_w_qkv(jax.random.fold_in(key_list[6], 71), 0),
        "w_out": bell_draw(key_list[4], (HEADS * DH, C), (HEADS * DH) ** -0.5, 0.15625, ((0, 8),)),
        "grad_out": bell_draw(key_list[5], (L, SEQS, C), 1.0, 6.0, ((0, 128),)),
    }


def rounded(value_matrix):
    return lax.optimization_barrier(value_matrix.astype(jnp.bfloat16)).astype(jnp.float32)

def broaden_heads(value_matrix):
    return value_matrix.astype(jnp.float32)

def head_forward(inputs):
    query_matrix, key_matrix, value_matrix = inputs
    logit_scale = DH ** (-0.5)
    attention_logits = jnp.einsum('ype,tpe->pyt', broaden_heads(query_matrix), broaden_heads(key_matrix), precision=lax.Precision.HIGHEST) * logit_scale
    row_peak = lax.optimization_barrier(jnp.max(attention_logits, axis=-1, keepdims=True))
    exponent = jnp.exp(attention_logits - row_peak)
    row_total = lax.optimization_barrier(jnp.sum(exponent, axis=-1, keepdims=True))
    narrow_probabilities = rounded(exponent / row_total)
    attention_output = jnp.einsum('wlc,cwy->lwy', narrow_probabilities, broaden_heads(value_matrix), precision=lax.Precision.HIGHEST)
    return (attention_output, (row_peak + jnp.log(row_total))[..., 0])

def head_back(inputs):
    query_matrix, key_matrix, value_matrix, d_out, attention_output, log_total = inputs
    logit_scale = DH ** (-0.5)
    wide_query_matrix = broaden_heads(query_matrix)
    wide_key_matrix = broaden_heads(key_matrix)
    wide_output_gradient = broaden_heads(d_out)
    attention_logits = jnp.einsum('ype,tpe->pyt', wide_query_matrix, wide_key_matrix, precision=lax.Precision.HIGHEST) * logit_scale
    soft_back = jnp.exp(attention_logits - log_total[..., None])
    probability_gradient = jnp.einsum('ype,tpe->pyt', wide_output_gradient, broaden_heads(value_matrix), precision=lax.Precision.HIGHEST)
    delta = lax.optimization_barrier(jnp.sum(wide_output_gradient * attention_output, axis=-1))
    d_scores = soft_back * (probability_gradient - jnp.transpose(delta)[..., None])
    narrow_gradient = rounded(d_scores)
    narrow_probabilities = rounded(soft_back)
    query_gradient = logit_scale * jnp.einsum('wlc,cwy->lwy', narrow_gradient, wide_key_matrix, precision=lax.Precision.HIGHEST)
    ds_blocks = narrow_gradient.reshape(SEQS, N_SEQ, BLOCK, L)
    soft_blocks = narrow_probabilities.reshape(SEQS, N_SEQ, BLOCK, L)
    query_blocks = wide_query_matrix.reshape(N_SEQ, BLOCK, SEQS, DH)
    dout_blocks = wide_output_gradient.reshape(N_SEQ, BLOCK, SEQS, DH)
    key_parts = logit_scale * jnp.einsum('bnqk,nqbd->nkbd', ds_blocks, query_blocks, precision=lax.Precision.HIGHEST)
    value_parts = jnp.einsum('bnqk,nqbd->nkbd', soft_blocks, dout_blocks, precision=lax.Precision.HIGHEST)
    d_keys = lax.optimization_barrier(jnp.sum(rounded(key_parts), axis=0))
    d_values = lax.optimization_barrier(jnp.sum(rounded(value_parts), axis=0))
    return jnp.stack([query_gradient, d_keys, d_values])

def split_heads(array):
    return jnp.transpose(array.reshape(array.shape[0], array.shape[1], HEADS, DH), (2, 0, 1, 3))

def join_heads(array):
    return jnp.transpose(array, (1, 2, 0, 3)).reshape(array.shape[1], array.shape[2], HEADS * DH)

def reference(enc_in, conv_weight, norm_gain, w_qkv, w_out, grad_out):
    padded = jnp.pad(enc_in, ((2, 2), (0, 0), (0, 0)))
    convolved = jnp.zeros((LF, SEQS, C), jnp.float32)
    for offset in range(KW):
        convolved = convolved + jnp.einsum('tbi,io->tbo', broaden_heads(padded[offset:offset + LF]), broaden_heads(conv_weight[offset]))
    activated, gelu_pull = jax.vjp(jax.nn.gelu, convolved)
    skip = lax.optimization_barrier(jnp.mean(activated.reshape(L, 2, SEQS, C), axis=1)).astype(jnp.bfloat16)
    skip_wide = broaden_heads(skip)
    inv_rms = lax.rsqrt(lax.optimization_barrier(jnp.mean(skip_wide * skip_wide, axis=-1, keepdims=True)) + 1e-06)
    normed = (skip_wide * inv_rms * norm_gain).astype(jnp.bfloat16)
    normed_wide = broaden_heads(normed)
    qkv = jnp.einsum('tbc,ice->itbe', normed_wide, broaden_heads(w_qkv)).astype(jnp.bfloat16)
    query_matrix, key_matrix, value_matrix = (split_heads(qkv[0]), split_heads(qkv[1]), split_heads(qkv[2]))
    attention_output, log_total = lax.map(head_forward, (query_matrix, key_matrix, value_matrix))
    o_narrow = join_heads(attention_output).astype(jnp.bfloat16)
    o_wide = broaden_heads(o_narrow)
    out_wide = broaden_heads(w_out)
    qkv_wide = broaden_heads(w_qkv)
    group_width = HEADS_DEV * DH
    head_sum = jnp.zeros((L, SEQS, C), jnp.float32)
    for head_group in range(N_HEAD):
        first = head_group * group_width
        term = jnp.einsum('tbe,ec->tbc', o_wide[:, :, first:first + group_width], out_wide[first:first + group_width])
        head_sum = head_sum + rounded(term)
    mixed = (skip_wide + head_sum).astype(jnp.bfloat16)
    grad_wide = broaden_heads(grad_out)
    grad_w_out = jnp.einsum('tbe,tbc->ec', o_wide, grad_wide)
    d_out = jnp.einsum('tbc,ec->tbe', grad_wide, out_wide).astype(jnp.bfloat16)
    grads = lax.map(head_back, (query_matrix, key_matrix, value_matrix, split_heads(d_out), attention_output, log_total))
    dqkv = jnp.stack([join_heads(grads[:, 0]), join_heads(grads[:, 1]), join_heads(grads[:, 2])]).astype(jnp.bfloat16)
    dqkv_wide = broaden_heads(dqkv)
    grad_w_qkv = jnp.einsum('tbc,itbe->ice', normed_wide, dqkv_wide)
    d_normed = jnp.zeros((L, SEQS, C), jnp.float32)
    for head_group in range(N_HEAD):
        first = head_group * group_width
        term = jnp.einsum('itbe,ice->tbc', dqkv_wide[:, :, :, first:first + group_width], qkv_wide[:, :, first:first + group_width])
        d_normed = d_normed + rounded(term)
    unit_rows = skip_wide * inv_rms
    scaled = d_normed * norm_gain
    d_skip = grad_wide + inv_rms * (scaled - unit_rows * lax.optimization_barrier(jnp.mean(scaled * unit_rows, axis=-1, keepdims=True)))
    d_act = jnp.repeat(d_skip, 2, axis=0) * 0.5
    d_conv = gelu_pull(d_act)[0].astype(jnp.bfloat16)
    d_pad = broaden_heads(jnp.pad(d_conv, ((2, 2), (0, 0), (0, 0))))
    grad_input = jnp.zeros((LF, SEQS, C_IN), jnp.float32)
    for offset in range(KW):
        grad_input = grad_input + jnp.einsum('tbo,io->tbi', d_pad[4 - offset:4 - offset + LF], broaden_heads(conv_weight[offset]))
    return (mixed, grad_input.astype(jnp.bfloat16), grad_w_qkv, grad_w_out)
```

```python
import math

import jax
import jax.numpy as jnp
from jax import lax
from jax.experimental import pallas as pl
from jax.experimental.pallas import tpu as pltpu
from jax.sharding import PartitionSpec as P

DH = 192
KW = 5
C = 1536
SCALE = DH ** (-0.5)
LOG2E = math.log2(math.e)
MESH = pl.DeviceIdType.MESH
F32 = jnp.float32
BF16 = jnp.bfloat16
VM = pltpu.VMEM


def coords():
    s = lax.axis_index("seq")
    h = lax.axis_index("head")
    return s // 4, (s // 2) % 2, s % 2, h // 4, h % 4


def device(y, zh, c, zl, x):
    return (y * 4 + zh * 2 + c, zl * 4 + x)


def x_peers():
    y, zh, c, zl, x = coords()
    return [device(y, zh, c, zl, (x + d) % 4) for d in (1, 2, 3)]


def zl_peer():
    y, zh, c, zl, x = coords()
    return device(y, zh, c, 1 - zl, x)


def core_peer():
    y, zh, c, zl, x = coords()
    return device(y, zh, 1 - c, zl, x)


def y_pair_peer():
    y, zh, c, zl, x = coords()
    return device(y + 1 - 2 * (y % 2), zh, c, zl, x)


def group():
    y, zh, c, zl, x = coords()
    return (y // 2) * 2 + zh


def group_peers():
    y, zh, c, zl, x = coords()
    peers = []
    for dy, dz in ((0, 1), (1, 0), (1, 1)):
        yh = (y // 2 + dy) % 2
        z2 = (zh + dz) % 2
        peers.append((yh * 2 + z2, device(yh * 2 + y % 2, z2, c, zl, x)))
    return peers


def barrier(peers):
    sem = pltpu.get_barrier_semaphore()
    for peer in peers:
        pl.semaphore_signal(sem, inc=1, device_id=peer, device_id_type=MESH)
    pl.semaphore_wait(sem, len(peers))


class Links:
    def __init__(self, send, recv):
        self.send, self.recv, self.used, self.all = send, recv, 0, []

    def start(self, src, dst, peer):
        copy = pltpu.make_async_remote_copy(
            src_ref=src,
            dst_ref=dst,
            send_sem=self.send.at[self.used],
            recv_sem=self.recv.at[self.used],
            device_id=peer,
            device_id_type=MESH,
        )
        self.used += 1
        self.all.append(copy)
        copy.start()
        return copy

    def finish(self):
        for copy in self.all:
            copy.wait_send()


def nt(a, b):
    return lax.dot_general(a, b, (((1,), (1,)), ((), ())), preferred_element_type=F32)


def nn(a, b):
    return lax.dot_general(a, b, (((1,), (0,)), ((), ())), preferred_element_type=F32)


class Gather:
    def __init__(self, links, buf):
        self.links, self.buf = links, buf
        y, zh, c, zl, x = coords()
        self.me = zl * 4 + x
        self.zl, self.x = zl, x

    def begin(self):
        own = self.buf.at[self.me]
        self.to_z = self.links.start(own, own, zl_peer())
        self.to_x = [self.links.start(own, own, peer) for peer in x_peers()]

    def forward(self):
        self.to_z.wait_recv()
        part = self.buf.at[(1 - self.zl) * 4 + self.x, pl.ds(0, 2)]
        self.fwd_x = [self.links.start(part, part, peer) for peer in x_peers()]
        self.fwd_z = []
        for d, copy in zip((1, 2, 3), self.to_x):
            copy.wait_recv()
            part = self.buf.at[self.zl * 4 + (self.x + 4 - d) % 4, pl.ds(2, 2)]
            self.fwd_z.append(self.links.start(part, part, zl_peer()))

    def end(self):
        for copy in self.fwd_x + self.fwd_z:
            copy.wait_recv()


def exchange_in(links, slab, buf, me):
    mine = group()
    buf[me, mine] = slab[mine]
    return [links.start(slab.at[g], buf.at[me, mine], peer) for g, peer in group_peers()]


class Scatter:
    def __init__(self, links, terms, first, second, last, pair, pair_sum, third, final):
        self.links, self.terms = links, terms
        self.first, self.second, self.last = first, second, last
        self.pair, self.pair_sum, self.third, self.final = pair, pair_sum, third, final
        y, zh, c, zl, x = coords()
        self.zl, self.x = zl, x
        self.me = zl * 4 + x

    def begin(self):
        zl, x, links = self.zl, self.x, self.links
        other = 1 - zl
        low, high = pl.ds(0, 64), pl.ds(64, 64)
        self.c_pair = [
            links.start(self.terms.at[other * 4 + k, high], self.pair.at[k], zl_peer()) for k in range(4)
        ]
        self.c_second = [
            links.start(self.terms.at[other * 4 + (x + d) % 4, low], self.second.at[d - 1], peer)
            for d, peer in zip((1, 2, 3), x_peers())
        ]
        self.c_first = [
            links.start(self.terms.at[zl * 4 + (x + d) % 4, low], self.first.at[d - 1], peer)
            for d, peer in zip((1, 2, 3), x_peers())
        ]

    def middle(self):
        zl, x, links = self.zl, self.x, self.links
        low, high = pl.ds(0, 64), pl.ds(64, 64)
        for copy in self.c_pair:
            copy.wait_recv()

        def add_pair(k, carry):
            self.pair_sum[k] = (
                self.terms[zl * 4 + k, high].astype(F32) + self.pair[k].astype(F32)
            ).astype(BF16)
            return carry

        lax.fori_loop(0, 4, add_pair, 0)
        self.c_third = [
            links.start(self.pair_sum.at[(x + d) % 4], self.third.at[d - 1], peer)
            for d, peer in zip((1, 2, 3), x_peers())
        ]
        for copy in self.c_second:
            copy.wait_recv()
        total = self.terms[(1 - zl) * 4 + x, low].astype(F32)
        for k in range(3):
            total = total + self.second[k].astype(F32)
        self.second[3] = total.astype(BF16)
        self.c_last = links.start(self.second.at[3], self.last, zl_peer())

    def end(self):
        zl, x = self.zl, self.x
        low = pl.ds(0, 64)
        for copy in self.c_first + self.c_third + [self.c_last]:
            copy.wait_recv()
        total = self.terms[self.me, low].astype(F32) + self.last[...].astype(F32)
        for k in range(3):
            total = total + self.first[k].astype(F32)
        self.final[0:2] = total.astype(BF16).reshape(2, 32, C)
        total = self.pair_sum[x].astype(F32)
        for k in range(3):
            total = total + self.third[k].astype(F32)
        self.final[2:4] = total.astype(BF16).reshape(2, 32, C)


SCATTER_SCRATCH = [
    VM((3, 64, C), BF16),
    VM((4, 64, C), BF16),
    VM((64, C), BF16),
    VM((4, 64, C), BF16),
    VM((4, 64, C), BF16),
    VM((3, 64, C), BF16),
    VM((4, 32, C), BF16),
]


def exchange_out(links, final, out):
    mine = group()
    out[mine] = final[mine]
    return [links.start(final.at[g], out.at[mine], peer) for g, peer in group_peers()]


def rows_of(ref, i):
    return ref[pl.ds(2 * i, 2)].reshape(256, C)


def gather_kernel(normed, grad, w, x_all, g_own, q, qt, kvt, send, recv):
    y, zh, c, zl, x = coords()
    me = zl * 4 + x
    barrier(x_peers() + [zl_peer()] + [peer for _, peer in group_peers()])
    links = Links(send, recv)
    copies = exchange_in(links, normed, x_all, me)
    for copy in copies:
        copy.wait_recv()
    gather = Gather(links, x_all)
    gather.begin()
    mine = group()
    g_own[mine] = grad[mine]
    copies = [links.start(grad.at[g], g_own.at[mine], peer) for g, peer in group_peers()]
    gather.forward()
    gather.end()

    def project(i, carry):
        rows = rows_of(x_all, i)
        part = nt(rows, w[0:DH])
        q[i] = part.astype(BF16)
        columns = pl.ds(pl.multiple_of(i * 256, 256), 256)
        qt[:, columns] = jnp.transpose(part).astype(BF16)
        kvt[:, columns] = nt(w[DH : 3 * DH], rows).astype(BF16)
        return carry

    lax.fori_loop(0, 4, project, 0)
    for copy in copies:
        copy.wait_recv()
    links.finish()


def attention_kernel(
    g_own, q, qt, kvt, w_out,
    mixed_out, gwo, dq_out, dqt_out, dkv_out,
    send, recv, g_all, kv, peak, chunk_peak, total, o_acc, e_all, ob, ot, do, dot_, delta,
    ds, dq_acc, acc, dkv_send, dkv_recv, terms, s1, s2, s3, s4, s5, s6, s7,
):
    y, zh, c, zl, x = coords()
    me = zl * 4 + x
    barrier(
        x_peers() + [zl_peer(), core_peer(), y_pair_peer()] + [peer for _, peer in group_peers()]
    )
    links = Links(send, recv)
    kv[0] = kvt[...]
    to_pair = links.start(kvt, kv.at[2], y_pair_peer())
    to_core = links.start(kvt, kv.at[1], core_peer())
    g_all[me] = g_own[...]
    gather = Gather(links, g_all)
    gather.begin()

    peak[...] = jnp.full_like(peak, -jnp.inf)
    total[...] = jnp.zeros_like(total)
    o_acc[...] = jnp.zeros_like(o_acc)
    unit = SCALE * LOG2E

    def forward(j):
        def tile(i, carry):
            s = nn(q[i], kv[j, 0:DH])
            old = peak[i]
            new = jnp.maximum(old, jnp.max(s, axis=-1, keepdims=True))
            peak[i] = new
            chunk_peak[j, i] = new
            fade = jnp.exp2((old - new) * unit)
            e = jnp.exp2(s * unit - new * unit)
            total[i] = total[i] * fade + jnp.sum(e, axis=-1, keepdims=True)
            eb = e.astype(BF16)
            e_all[j, i] = eb
            o_acc[i] = o_acc[i] * fade + nt(eb, kv[j, DH : 2 * DH])
            return carry

        lax.fori_loop(0, 4, tile, 0)

    forward(0)
    to_core.wait_recv()
    forward(1)
    to_pair.wait_recv()
    relay = links.start(kv.at[2], kv.at[3], core_peer())
    gather.forward()
    forward(2)
    relay.wait_recv()
    forward(3)

    def finish_tile(i, carry):
        inverse = 1.0 / total[i]
        o = o_acc[i] * inverse
        o_acc[i] = o
        ob[i] = o.astype(BF16)
        ot[:, pl.ds(pl.multiple_of(i * 256, 256), 256)] = jnp.transpose(o).astype(BF16)
        for j in range(4):
            chunk_peak[j, i] = jnp.exp2((chunk_peak[j, i] - peak[i]) * unit) * inverse
        term = nn(ob[i], w_out[...]).astype(BF16)
        terms[pl.ds(2 * i, 2)] = term.reshape(2, 128, C)
        return carry

    lax.fori_loop(0, 4, finish_tile, 0)
    scatter = Scatter(links, terms, s1, s2, s3, s4, s5, s6, s7)
    gather.end()
    scatter.begin()

    def output_gradient(i, carry):
        d = nt(rows_of(g_all, i), w_out[...])
        db = d.astype(BF16)
        do[i] = db
        db = db.astype(F32)
        dot_[:, pl.ds(pl.multiple_of(i * 256, 256), 256)] = jnp.transpose(db).astype(BF16)
        delta[i] = jnp.sum(db * o_acc[i], axis=-1, keepdims=True)
        dq_acc[i] = jnp.zeros((256, DH), F32)
        return carry

    lax.fori_loop(0, 4, output_gradient, 0)

    def backward(j):
        def tile(i, carry):
            p = e_all[j, i].astype(F32) * chunk_peak[j, i]
            e_all[j, i] = p.astype(BF16)
            dp = nn(do[i], kv[j, DH : 2 * DH])
            d = (p * (dp - delta[i])).astype(BF16)
            ds[i] = d
            dq_acc[i] += nt(d, kv[j, 0:DH])
            return carry

        lax.fori_loop(0, 4, tile, 0)

        def columns(n, carry):
            cut = pl.ds(pl.multiple_of(n * 256, 256), 256)
            acc[0:DH, cut] = nn(qt[...], ds[:, :, cut].reshape(1024, 256)) * SCALE
            acc[DH : 2 * DH, cut] = nn(dot_[...], e_all[j, :, :, cut].reshape(1024, 256))
            return carry

        lax.fori_loop(0, 4, columns, 0)

    backward(3)
    dkv_send[0] = acc[...].astype(BF16)
    far = links.start(dkv_send.at[0], dkv_recv.at[0], core_peer())
    backward(2)
    far.wait_recv()
    dkv_send[1] = (acc[...] + dkv_recv[0].astype(F32)).astype(BF16)
    pair = links.start(dkv_send.at[1], dkv_recv.at[1], y_pair_peer())
    backward(1)
    dkv_send[2] = acc[...].astype(BF16)
    near = links.start(dkv_send.at[2], dkv_recv.at[2], core_peer())
    scatter.middle()
    backward(0)

    def query(i, carry):
        d = dq_acc[i] * SCALE
        dq_out[i] = d.astype(BF16)
        dqt_out[:, pl.ds(pl.multiple_of(i * 256, 256), 256)] = jnp.transpose(d).astype(BF16)
        return carry

    lax.fori_loop(0, 4, query, 0)

    def w_out_gradient(n, carry):
        cut = pl.ds(pl.multiple_of(n * 512, 512), 512)
        gwo[:, cut] = nn(ot[...], g_all[:, :, :, cut].reshape(1024, 512)).astype(BF16)
        return carry

    lax.fori_loop(0, 3, w_out_gradient, 0)
    scatter.end()
    out = exchange_out(links, s7, mixed_out)
    near.wait_recv()
    pair.wait_recv()
    dkv_out[...] = (acc[...] + dkv_recv[1].astype(F32) + dkv_recv[2].astype(F32)).astype(BF16)
    for copy in out:
        copy.wait_recv()
    links.finish()


def chip_peers():
    y, zh, c, zl, x = coords()
    me = y * 2 + zh
    peers = []
    for d in range(1, 8):
        k = (me + d) % 8
        peers.append((k, device(k // 2, k % 2, c, zl, x)))
    return peers


def gradient_kernel(
    x_all, dq, dqt, dkv, w, gwo,
    normed_out, weights_out,
    send, recv, dkv_rows, terms, s1, s2, s3, s4, s5, s6, s7, part, half_in, half, piece_in, done,
):
    y, zh, c, zl, x = coords()
    me = zl * 4 + x
    chip = y * 2 + zh
    barrier(x_peers() + [zl_peer(), core_peer()] + [peer for _, peer in chip_peers()])
    links = Links(send, recv)

    def flip(i, carry):
        cut = pl.ds(pl.multiple_of(i * 256, 256), 256)
        dkv_rows[i] = jnp.transpose(dkv[:, cut].astype(F32)).astype(BF16)
        return carry

    lax.fori_loop(0, 4, flip, 0)

    def term(i, carry):
        t = nn(dq[i], w[0:DH]) + nn(dkv_rows[i], w[DH : 3 * DH])
        terms[pl.ds(2 * i, 2)] = t.astype(BF16).reshape(2, 128, C)
        return carry

    lax.fori_loop(0, 4, term, 0)
    scatter = Scatter(links, terms, s1, s2, s3, s4, s5, s6, s7)
    scatter.begin()

    def weights(n, carry):
        cut = pl.ds(pl.multiple_of(n * 512, 512), 512)
        rows = x_all[:, :, :, cut].reshape(1024, 512)
        part[0:4, :, cut] = nn(dqt[...], rows).astype(BF16).reshape(4, 48, 512)
        part[4:12, :, cut] = nn(dkv[...], rows).astype(BF16).reshape(8, 48, 512)
        part[12:16, :, cut] = gwo[:, cut].reshape(4, 48, 512)
        return carry

    lax.fori_loop(0, 3, weights, 0)
    swap = links.start(part.at[pl.ds((1 - c) * 8, 8)], half_in, core_peer())
    swap.wait_recv()

    def add_half(k, carry):
        half[k] = (part[c * 8 + k].astype(F32) + half_in[k].astype(F32)).astype(BF16)
        return carry

    lax.fori_loop(0, 8, add_half, 0)
    pieces = [
        links.start(half.at[k], piece_in.at[n], peer) for n, (k, peer) in enumerate(chip_peers())
    ]
    scatter.middle()
    for copy in pieces:
        copy.wait_recv()
    total = half[chip].astype(F32)
    for n in range(7):
        total = total + piece_in[n].astype(F32)
    done[c, chip] = total.astype(BF16)
    spread = [links.start(done.at[c, chip], done.at[c, chip], peer) for _, peer in chip_peers()]
    scatter.end()
    out = exchange_out(links, s7, normed_out)
    for copy in spread:
        copy.wait_recv()
    mirror = links.start(done.at[c], done.at[c], core_peer())
    mirror.wait_recv()

    def widen(k, carry):
        weights_out[k] = done[k // 8, k % 8].astype(F32)
        return carry

    lax.fori_loop(0, 16, widen, 0)
    for copy in out:
        copy.wait_recv()
    links.finish()


def vmem_call(kernel, collective_id, inputs, outputs, scratch, limit, copies):
    spec = pl.BlockSpec(memory_space=VM)
    return pl.pallas_call(
        kernel,
        out_shape=[jax.ShapeDtypeStruct(shape, dtype) for shape, dtype in outputs],
        in_specs=[spec] * len(inputs),
        out_specs=[spec] * len(outputs),
        scratch_shapes=[pltpu.SemaphoreType.DMA((copies,)), pltpu.SemaphoreType.DMA((copies,))] + scratch,
        compiler_params=pltpu.CompilerParams(
            collective_id=collective_id, has_side_effects=True, vmem_limit_bytes=limit << 20
        ),
    )(*inputs)


def shift_halo(low_rows, high_rows):
    forward = [(i, i + 1) for i in range(127)]
    backward = [(target, source) for source, target in forward]
    axes = ("seq", "head")
    return lax.ppermute(high_rows, axes, forward), lax.ppermute(low_rows, axes, backward)


def padded_2(block):
    low, high = shift_halo(block[:, :2], block[:, -2:])
    return jnp.concatenate([low, block, high], axis=1)


def body(enc_in, conv_weight, norm_gain, w_qkv, w_out, grad_out):
    enc = jnp.transpose(enc_in, (1, 0, 2))
    grad = jnp.transpose(grad_out, (1, 0, 2))
    w = jnp.transpose(w_qkv, (0, 2, 1)).reshape(3 * DH, C)
    padded = padded_2(enc)
    convolved = jnp.zeros((4, 64, C), F32)
    for offset in range(KW):
        convolved = convolved + jnp.einsum(
            "bti,io->bto", padded[:, offset : offset + 64], conv_weight[offset], preferred_element_type=F32
        )
    activated, gelu_pull = jax.vjp(jax.nn.gelu, convolved)
    skip = jnp.mean(activated.reshape(4, 32, 2, C), axis=2).astype(BF16)
    skip_wide = skip.astype(F32)
    inv_rms = lax.rsqrt(jnp.mean(skip_wide * skip_wide, axis=-1, keepdims=True) + 1e-06)
    normed = (skip_wide * inv_rms * norm_gain).astype(BF16)

    x_all, g_own, q, qt, kvt = vmem_call(
        gather_kernel,
        0,
        [normed, grad, w],
        [
            ((8, 4, 32, C), BF16),
            ((4, 32, C), BF16),
            ((4, 256, DH), BF16),
            ((DH, 1024), BF16),
            ((2 * DH, 1024), BF16),
        ],
        [],
        30,
        16,
    )
    head_sum, gwo, dq, dqt, dkv = vmem_call(
        attention_kernel,
        1,
        [g_own, q, qt, kvt, w_out],
        [
            ((4, 32, C), BF16),
            ((DH, C), BF16),
            ((4, 256, DH), BF16),
            ((DH, 1024), BF16),
            ((2 * DH, 1024), BF16),
        ],
        [
            VM((8, 4, 32, C), BF16),
            VM((4, 2 * DH, 1024), BF16),
            VM((4, 256, 1), F32),
            VM((4, 4, 256, 1), F32),
            VM((4, 256, 1), F32),
            VM((4, 256, DH), F32),
            VM((4, 4, 256, 1024), BF16),
            VM((4, 256, DH), BF16),
            VM((DH, 1024), BF16),
            VM((4, 256, DH), BF16),
            VM((DH, 1024), BF16),
            VM((4, 256, 1), F32),
            VM((4, 256, 1024), BF16),
            VM((4, 256, DH), F32),
            VM((2 * DH, 1024), F32),
            VM((3, 2 * DH, 1024), BF16),
            VM((3, 2 * DH, 1024), BF16),
            VM((8, 128, C), BF16),
        ]
        + SCATTER_SCRATCH,
        58,
        36,
    )
    d_normed, weights = vmem_call(
        gradient_kernel,
        2,
        [x_all, dq, dqt, dkv, w, gwo],
        [((4, 32, C), BF16), ((16, 48, C), F32)],
        [VM((4, 256, 2 * DH), BF16), VM((8, 128, C), BF16)]
        + SCATTER_SCRATCH
        + [
            VM((16, 48, C), BF16),
            VM((8, 48, C), BF16),
            VM((8, 48, C), BF16),
            VM((7, 48, C), BF16),
            VM((2, 8, 48, C), BF16),
        ],
        50,
        40,
    )
    mixed = (skip_wide + head_sum.astype(F32)).astype(BF16)
    d_normed = d_normed.astype(F32)
    unit_rows = skip_wide * inv_rms
    scaled = d_normed * norm_gain
    d_skip = grad.astype(F32) + inv_rms * (
        scaled - unit_rows * jnp.mean(scaled * unit_rows, axis=-1, keepdims=True)
    )
    d_act = jnp.repeat(d_skip, 2, axis=1) * 0.5
    d_conv = gelu_pull(d_act)[0].astype(BF16)
    d_pad = padded_2(d_conv)
    grad_input = jnp.zeros((4, 64, enc_in.shape[2]), F32)
    for offset in range(KW):
        grad_input = grad_input + jnp.einsum(
            "bto,io->bti",
            d_pad[:, 4 - offset : 4 - offset + 64],
            conv_weight[offset],
            preferred_element_type=F32,
        )
    weights = weights.reshape(4 * DH, C)
    return (
        jnp.transpose(mixed, (1, 0, 2)),
        jnp.transpose(grad_input.astype(BF16), (1, 0, 2)),
        jnp.transpose(weights[: 3 * DH].reshape(3, DH, C), (0, 2, 1)),
        weights[3 * DH :],
    )


def solution(mesh):
    return jax.shard_map(
        body,
        mesh=mesh,
        in_specs=(
            P(("seq", "head"), None, None),
            P(),
            P(),
            P(None, None, "head"),
            P("head", None),
            P(("seq", "head"), None, None),
        ),
        out_specs=(
            P(("seq", "head"), None, None),
            P(("seq", "head"), None, None),
            P(None, None, "head"),
            P("head", None),
        ),
        check_vma=False,
    )
```

```python
import math

import jax
import jax.numpy as jnp
from jax import lax
from jax.experimental import pallas as pl
from jax.experimental.pallas import tpu as pltpu
from jax.sharding import PartitionSpec as P

DH = 192
KW = 5
C = 1536
SCALE = DH ** (-0.5)
LOG2E = math.log2(math.e)
MESH = pl.DeviceIdType.MESH
F32 = jnp.float32
BF16 = jnp.bfloat16
VM = pltpu.VMEM


def coords():
    s = lax.axis_index("seq")
    h = lax.axis_index("head")
    return s // 4, (s // 2) % 2, s % 2, h // 4, h % 4


def device(y, zh, c, zl, x):
    return (y * 4 + zh * 2 + c, zl * 4 + x)


def x_peers():
    y, zh, c, zl, x = coords()
    return [device(y, zh, c, zl, (x + d) % 4) for d in (1, 2, 3)]


def zl_peer():
    y, zh, c, zl, x = coords()
    return device(y, zh, c, 1 - zl, x)


def core_peer():
    y, zh, c, zl, x = coords()
    return device(y, zh, 1 - c, zl, x)


def y_pair_peer():
    y, zh, c, zl, x = coords()
    return device(y + 1 - 2 * (y % 2), zh, c, zl, x)


def group():
    y, zh, c, zl, x = coords()
    return (y // 2) * 2 + zh


def group_peers():
    y, zh, c, zl, x = coords()
    peers = []
    for dy, dz in ((0, 1), (1, 0), (1, 1)):
        yh = (y // 2 + dy) % 2
        z2 = (zh + dz) % 2
        peers.append((yh * 2 + z2, device(yh * 2 + y % 2, z2, c, zl, x)))
    return peers


def greet(peers):
    sem = pltpu.get_barrier_semaphore()
    for peer in peers:
        pl.semaphore_signal(sem, inc=1, device_id=peer, device_id_type=MESH)
    return len(peers)


def met(count):
    pl.semaphore_wait(pltpu.get_barrier_semaphore(), count)


class Links:
    def __init__(self, send, recv):
        self.send, self.recv, self.used, self.all = send, recv, 0, []

    def start(self, src, dst, peer):
        copy = pltpu.make_async_remote_copy(
            src_ref=src,
            dst_ref=dst,
            send_sem=self.send.at[self.used],
            recv_sem=self.recv.at[self.used],
            device_id=peer,
            device_id_type=MESH,
        )
        self.used += 1
        self.all.append(copy)
        copy.start()
        return copy

    def finish(self):
        for copy in self.all:
            copy.wait_send()


def nt(a, b):
    return lax.dot_general(a, b, (((1,), (1,)), ((), ())), preferred_element_type=F32)


def nn(a, b):
    return lax.dot_general(a, b, (((1,), (0,)), ((), ())), preferred_element_type=F32)


def x_neighbours():
    y, zh, c, zl, x = coords()
    return device(y, zh, c, zl, (x + 1) % 4), device(y, zh, c, zl, (x + 3) % 4)


class Gather:
    def __init__(self, links, buf):
        self.links, self.buf = links, buf
        y, zh, c, zl, x = coords()
        self.zl, self.x = zl, x
        self.order = [group()] + [g for g, _ in group_peers()]

    def at(self, plane, dx, r):
        return self.buf.at[plane * 4 + (self.x + dx) % 4, self.order[r]]

    def begin(self, incoming):
        up, down = x_neighbours()
        start = self.links.start
        self.up, self.down, self.z = {}, {}, {}
        for r in range(4):
            if r > 0 and incoming is not None:
                incoming[r - 1].wait_recv()
            own = self.at(self.zl, 0, r)
            self.up[r] = start(own, own, up)
            self.down[r] = start(own, own, down)
            self.z[r] = start(own, own, zl_peer())

    def forward(self):
        up, down = x_neighbours()
        z, zl, other = zl_peer(), self.zl, 1 - self.zl
        self.rest = []

        def send(part, peer):
            return self.links.start(part, part, peer)

        self.up[0].wait_recv()
        self.relay_0 = send(self.at(zl, 3, 0), up)
        self.rest.append(send(self.at(zl, 3, 0), z))
        self.down[1].wait_recv()
        self.relay_1 = send(self.at(zl, 1, 1), down)
        self.rest.append(send(self.at(zl, 1, 1), z))
        self.z[2].wait_recv()
        self.over_2 = send(self.at(other, 0, 2), up)
        self.rest.append(send(self.at(other, 0, 2), down))
        self.z[3].wait_recv()
        self.over_3 = send(self.at(other, 0, 3), down)
        self.rest.append(send(self.at(other, 0, 3), up))
        self.down[0].wait_recv()
        self.rest.append(send(self.at(zl, 1, 0), z))
        self.up[1].wait_recv()
        self.rest.append(send(self.at(zl, 3, 1), z))
        self.up[2].wait_recv()
        self.rest.append(send(self.at(zl, 3, 2), up))
        self.down[3].wait_recv()
        self.rest.append(send(self.at(zl, 1, 3), down))

    def relay(self):
        up, down = x_neighbours()
        z, zl, other = zl_peer(), self.zl, 1 - self.zl

        def send(part, peer):
            self.rest.append(self.links.start(part, part, peer))

        self.relay_0.wait_recv()
        send(self.at(zl, 2, 0), z)
        self.relay_1.wait_recv()
        send(self.at(zl, 2, 1), z)
        self.over_2.wait_recv()
        send(self.at(other, 3, 2), up)
        self.over_3.wait_recv()
        send(self.at(other, 1, 3), down)

    def end(self):
        for copy in self.rest + [self.up[3], self.down[2], self.z[0], self.z[1]]:
            copy.wait_recv()


def exchange_in(links, slab, buf, me):
    mine = group()
    buf[me, mine] = slab[mine]
    return [links.start(slab.at[g], buf.at[me, mine], peer) for g, peer in group_peers()]


class Scatter:
    def __init__(self, links, terms, first, second, last, pair, pair_sum, third, final):
        self.links, self.terms = links, terms
        self.first, self.second, self.last = first, second, last
        self.pair, self.pair_sum, self.third, self.final = pair, pair_sum, third, final
        y, zh, c, zl, x = coords()
        self.zl, self.x = zl, x
        self.me = zl * 4 + x

    def begin_other(self):
        zl, x, links = self.zl, self.x, self.links
        other = 1 - zl
        low, high = pl.ds(0, 64), pl.ds(64, 64)
        self.c_pair = [
            links.start(self.terms.at[other * 4 + k, high], self.pair.at[k], zl_peer()) for k in range(4)
        ]
        self.c_second = [
            links.start(self.terms.at[other * 4 + (x + d) % 4, low], self.second.at[d - 1], peer)
            for d, peer in zip((1, 2, 3), x_peers())
        ]

    def begin_own(self):
        zl, x, links = self.zl, self.x, self.links
        low = pl.ds(0, 64)
        self.c_first = [
            links.start(self.terms.at[zl * 4 + (x + d) % 4, low], self.first.at[d - 1], peer)
            for d, peer in zip((1, 2, 3), x_peers())
        ]

    def middle(self):
        zl, x, links = self.zl, self.x, self.links
        low, high = pl.ds(0, 64), pl.ds(64, 64)
        for copy in self.c_pair:
            copy.wait_recv()

        def add_pair(k, carry):
            self.pair_sum[k] = (
                self.terms[zl * 4 + k, high].astype(F32) + self.pair[k].astype(F32)
            ).astype(BF16)
            return carry

        lax.fori_loop(0, 4, add_pair, 0)
        self.c_third = [
            links.start(self.pair_sum.at[(x + d) % 4], self.third.at[d - 1], peer)
            for d, peer in zip((1, 2, 3), x_peers())
        ]
        for copy in self.c_second:
            copy.wait_recv()
        total = self.terms[(1 - zl) * 4 + x, low].astype(F32)
        for k in range(3):
            total = total + self.second[k].astype(F32)
        self.second[3] = total.astype(BF16)
        self.c_last = links.start(self.second.at[3], self.last, zl_peer())

    def end(self):
        zl, x = self.zl, self.x
        low = pl.ds(0, 64)
        for copy in self.c_first + self.c_third + [self.c_last]:
            copy.wait_recv()
        total = self.terms[self.me, low].astype(F32) + self.last[...].astype(F32)
        for k in range(3):
            total = total + self.first[k].astype(F32)
        self.final[0:2] = total.astype(BF16).reshape(2, 32, C)
        total = self.pair_sum[x].astype(F32)
        for k in range(3):
            total = total + self.third[k].astype(F32)
        self.final[2:4] = total.astype(BF16).reshape(2, 32, C)


SCATTER_SCRATCH = [
    VM((3, 64, C), BF16),
    VM((4, 64, C), BF16),
    VM((64, C), BF16),
    VM((4, 64, C), BF16),
    VM((4, 64, C), BF16),
    VM((3, 64, C), BF16),
    VM((4, 32, C), BF16),
]


def exchange_out(links, final, out):
    mine = group()
    out[mine] = final[mine]
    return [links.start(final.at[g], out.at[mine], peer) for g, peer in group_peers()]


def rows_of(ref, i):
    return ref[pl.ds(2 * i, 2)].reshape(256, C)


def slab_peers():
    me = lax.axis_index("seq") * 8 + lax.axis_index("head")
    after, before = (me + 1) % 128, (me + 127) % 128
    return (after // 8, after % 8), (before // 8, before % 8)


def shifted(block, edge, up, here):
    width = block.shape[-1]
    wide = block.astype(F32)
    place = lax.broadcasted_iota(jnp.int32, (128, width), 0) % 32
    fill = jnp.where(here, edge.astype(F32), 0.0)
    fill = jnp.concatenate([jnp.broadcast_to(fill[b : b + 1], (32, width)) for b in range(4)], axis=0)
    if up:
        return jnp.where(place == 31, fill, pltpu.roll(wide, 127, 0)).astype(BF16)
    return jnp.where(place == 0, fill, pltpu.roll(wide, 1, 0)).astype(BF16)


def gather_kernel(
    enc, edges, gain, grad, w, conv_w,
    skip, rstd, slope, x_all, g_own, q, qt, kvt,
    send, recv, w_sem, w_buf, halo, taps, normed,
):
    y, zh, c, zl, x = coords()
    me = zl * 4 + x
    slab = lax.axis_index("seq") * 8 + lax.axis_index("head")
    after, before = slab_peers()

    def tile_copy(n):
        cut = pl.ds(pl.multiple_of(n * 256, 256), 256)
        return pltpu.make_async_copy(conv_w.at[:, :, cut], w_buf.at[n], w_sem.at[n])

    for n in range(6):
        tile_copy(n).start()
    met(greet([*x_neighbours(), zl_peer(), after, before] + [peer for _, peer in group_peers()]))
    links = Links(send, recv)
    to_after = links.start(edges.at[1], halo.at[0], after)
    to_before = links.start(edges.at[0], halo.at[1], before)
    mine = group()
    even, odd = enc[0].reshape(128, 768), enc[1].reshape(128, 768)
    low, high = pl.ds(0, 128), pl.ds(128, 128)
    taps[2, low], taps[2, high] = even, odd
    taps[3, low], taps[1, high] = odd, even
    to_after.wait_recv()
    to_before.wait_recv()
    first, last = slab > 0, slab < 127
    even_before = shifted(even, halo[0, 0], False, first)
    odd_before = shifted(odd, halo[0, 1], False, first)
    even_after = shifted(even, halo[1, 0], True, last)
    odd_after = shifted(odd, halo[1, 1], True, last)
    taps[0, low], taps[0, high] = even_before, odd_before
    taps[1, low], taps[3, high] = odd_before, even_after
    taps[4, low], taps[4, high] = even_after, odd_after
    root = math.sqrt(2.0 / math.pi)

    def conv_tile(n, squares):
        tile_copy(n).wait()
        cut = pl.ds(pl.multiple_of(n * 256, 256), 256)
        v = nn(taps[0], w_buf[n, 0])
        for k in range(1, KW):
            v = v + nn(taps[k], w_buf[n, k])
        v2 = v * v
        t = jnp.tanh(root * v * (1.0 + 0.044715 * v2))
        half = 0.5 * (1.0 + t)
        act = v * half
        pull = half + 0.5 * v * (1.0 - t * t) * (root * (1.0 + 3.0 * 0.044715 * v2))
        slope[:, cut] = pull * 0.5
        s = ((act[0:128] + act[128:256]) * 0.5).astype(BF16)
        skip[:, :, cut] = s.reshape(4, 32, 256)
        s = s.astype(F32)
        return squares + jnp.sum(s * s, axis=-1, keepdims=True)

    squares = lax.fori_loop(0, 6, conv_tile, jnp.zeros((128, 1), F32))
    r = lax.rsqrt(squares / C + 1e-06)
    rstd[...] = r
    value = skip[...].reshape(128, C).astype(F32) * r * gain[...]
    normed[...] = value.astype(BF16).reshape(4, 32, C)
    copies = exchange_in(links, normed, x_all, me)
    gather = Gather(links, x_all)
    gather.begin(copies)
    g_own[mine] = grad[mine]
    copies = [links.start(grad.at[g], g_own.at[mine], peer) for g, peer in group_peers()]
    gather.forward()
    gather.relay()
    gather.end()

    def project(i, carry):
        rows = rows_of(x_all, i)
        part = nt(rows, w[0:DH])
        q[i] = part.astype(BF16)
        columns = pl.ds(pl.multiple_of(i * 256, 256), 256)
        qt[:, columns] = jnp.transpose(part).astype(BF16)
        kvt[:, columns] = nt(w[DH : 3 * DH], rows).astype(BF16)
        return carry

    lax.fori_loop(0, 4, project, 0)
    for copy in copies:
        copy.wait_recv()
    links.finish()


def attention_kernel(
    g_own, q, qt, kvt, w_out,
    mixed_out, gwo, dq_out, dqt_out, dkv_out,
    send, recv, g_all, kv, peak, chunk_peak, total, o_acc, e_all, ob, ot, do, dot_, delta,
    ds, dq_acc, acc, dkv_send, dkv_recv, terms, s1, s2, s3, s4, s5, s6,
):
    y, zh, c, zl, x = coords()
    me = zl * 4 + x
    met(greet(x_peers() + [zl_peer(), core_peer(), y_pair_peer()]))
    links = Links(send, recv)
    kv[0] = kvt[...]
    to_pair = links.start(kvt, kv.at[2], y_pair_peer())
    to_core = links.start(kvt, kv.at[1], core_peer())
    g_all[me] = g_own[...]
    gather = Gather(links, g_all)
    gather.begin(None)

    peak[...] = jnp.full_like(peak, -jnp.inf)
    total[...] = jnp.zeros_like(total)
    o_acc[...] = jnp.zeros_like(o_acc)
    unit = SCALE * LOG2E

    def forward(j):
        def tile(i, carry):
            s = nn(q[i], kv[j, 0:DH])
            old = peak[i]
            new = jnp.maximum(old, jnp.max(s, axis=-1, keepdims=True))
            peak[i] = new
            chunk_peak[j, i] = new
            fade = jnp.exp2((old - new) * unit)
            e = jnp.exp2(s * unit - new * unit)
            total[i] = total[i] * fade + jnp.sum(e, axis=-1, keepdims=True)
            eb = e.astype(BF16)
            e_all[j, i] = eb
            o_acc[i] = o_acc[i] * fade + nt(eb, kv[j, DH : 2 * DH])
            return carry

        lax.fori_loop(0, 4, tile, 0, unroll=True)

    forward(0)
    to_core.wait_recv()
    forward(1)
    gather.forward()
    to_pair.wait_recv()
    relay = links.start(kv.at[2], kv.at[3], core_peer())
    gather.relay()
    forward(2)
    relay.wait_recv()
    forward(3)

    def finish_tile(i, carry):
        inverse = 1.0 / total[i]
        o = o_acc[i] * inverse
        o_acc[i] = o
        ob[i] = o.astype(BF16)
        ot[:, pl.ds(pl.multiple_of(i * 256, 256), 256)] = jnp.transpose(o).astype(BF16)
        for j in range(4):
            chunk_peak[j, i] = jnp.exp2((chunk_peak[j, i] - peak[i]) * unit) * inverse
        term = nn(ob[i], w_out[...]).astype(BF16)
        terms[pl.ds(2 * i, 2)] = term.reshape(2, 128, C)
        return carry

    lax.fori_loop(0, 4, finish_tile, 0)
    scatter = Scatter(links, terms, s1, s2, s3, s4, s5, s6, mixed_out)
    gather.end()
    scatter.begin_other()
    scatter.begin_own()

    def output_gradient(i, carry):
        d = nt(rows_of(g_all, i), w_out[...])
        db = d.astype(BF16)
        do[i] = db
        db = db.astype(F32)
        dot_[:, pl.ds(pl.multiple_of(i * 256, 256), 256)] = jnp.transpose(db).astype(BF16)
        delta[i] = jnp.sum(db * o_acc[i], axis=-1, keepdims=True)
        dq_acc[i] = jnp.zeros((256, DH), F32)
        return carry

    lax.fori_loop(0, 4, output_gradient, 0)

    def backward(j):
        def tile(i, carry):
            p = e_all[j, i].astype(F32) * chunk_peak[j, i]
            e_all[j, i] = p.astype(BF16)
            dp = nn(do[i], kv[j, DH : 2 * DH])
            d = (p * (dp - delta[i])).astype(BF16)
            ds[i] = d
            dq_acc[i] += nt(d, kv[j, 0:DH])
            return carry

        lax.fori_loop(0, 4, tile, 0, unroll=True)

        def columns(n, carry):
            cut = pl.ds(pl.multiple_of(n * 256, 256), 256)
            acc[0:DH, cut] = nn(qt[...], ds[:, :, cut].reshape(1024, 256)) * SCALE
            acc[DH : 2 * DH, cut] = nn(dot_[...], e_all[j, :, :, cut].reshape(1024, 256))
            return carry

        lax.fori_loop(0, 4, columns, 0)

    backward(3)
    dkv_send[0] = acc[...].astype(BF16)
    far = links.start(dkv_send.at[0], dkv_recv.at[0], core_peer())
    backward(2)
    far.wait_recv()
    dkv_send[1] = (acc[...] + dkv_recv[0].astype(F32)).astype(BF16)
    pair = links.start(dkv_send.at[1], dkv_recv.at[1], y_pair_peer())
    backward(1)
    dkv_send[2] = acc[...].astype(BF16)
    near = links.start(dkv_send.at[2], dkv_recv.at[2], core_peer())
    scatter.middle()
    backward(0)

    def query(i, carry):
        d = dq_acc[i] * SCALE
        dq_out[i] = d.astype(BF16)
        dqt_out[:, pl.ds(pl.multiple_of(i * 256, 256), 256)] = jnp.transpose(d).astype(BF16)
        return carry

    lax.fori_loop(0, 4, query, 0)

    def w_out_gradient(n, carry):
        cut = pl.ds(pl.multiple_of(n * 512, 512), 512)
        gwo[:, cut] = nn(ot[...], g_all[:, :, :, cut].reshape(1024, 512)).astype(BF16)
        return carry

    lax.fori_loop(0, 3, w_out_gradient, 0)
    scatter.end()
    near.wait_recv()
    pair.wait_recv()
    dkv_out[...] = (acc[...] + dkv_recv[1].astype(F32) + dkv_recv[2].astype(F32)).astype(BF16)
    links.finish()


def y_peers():
    y, zh, c, zl, x = coords()
    return [((y + d) % 4, device((y + d) % 4, zh, c, zl, x)) for d in (1, 2, 3)]


def zh_peer():
    y, zh, c, zl, x = coords()
    return device(y, 1 - zh, c, zl, x)


class Sum:
    def __init__(self, links, part, half_in, half, y_in, z_in, done):
        self.links, self.part, self.half_in, self.half = links, part, half_in, half
        self.y_in, self.z_in, self.done = y_in, z_in, done
        self.y, zh, self.c, zl, x = coords()

    def swap(self):
        self.c_swap = self.links.start(self.part.at[1 - self.c], self.half_in, core_peer())

    def over_y(self):
        self.c_swap.wait_recv()

        def add(k, carry):
            self.half[k] = (self.part[self.c, k].astype(F32) + self.half_in[k].astype(F32)).astype(BF16)
            return carry

        lax.fori_loop(0, 4, add, 0)
        self.c_y = [
            self.links.start(self.half.at[k], self.y_in.at[n], peer) for n, (k, peer) in enumerate(y_peers())
        ]

    def over_z(self):
        for copy in self.c_y:
            copy.wait_recv()
        total = self.half[self.y].astype(F32)
        for n in range(3):
            total = total + self.y_in[n].astype(F32)
        self.z_in[0] = total.astype(BF16)
        self.c_z = self.links.start(self.z_in.at[0], self.z_in.at[1], zh_peer())

    def spread(self):
        self.c_z.wait_recv()
        total = self.z_in[0].astype(F32) + self.z_in[1].astype(F32)
        self.done[self.c, self.y] = total.astype(BF16)
        piece = self.done.at[self.c, self.y]
        self.c_spread = [self.links.start(piece, piece, peer) for _, peer in y_peers()]

    def mirror(self):
        for copy in self.c_spread:
            copy.wait_recv()
        rows = self.done.at[self.c]
        self.c_mirror = self.links.start(rows, rows, core_peer())

    def end(self):
        self.c_mirror.wait_recv()


SUM_SCRATCH = [
    VM((2, 4, 48, C), BF16),
    VM((4, 48, C), BF16),
    VM((4, 48, C), BF16),
    VM((3, 48, C), BF16),
    VM((2, 48, C), BF16),
    VM((2, 4, 48, C), BF16),
]


def gradient_kernel(
    x_all, dq, dqt, dkv, w, gwo, mixed_in, skip, rstd, gain, slope, grad, conv_w,
    mixed_out, gw_out, gwo_out, grad_input,
    send, recv, w_sem, dkv_rows, terms, s1, s2, s3, s4, s5, s6, s7,
    a1, a2, a3, a4, a5, a6, b1, b2, b3, b4, b5, b6, w_buf, d_normed, edges, halo, taps,
):
    y, zh, c, zl, x = coords()
    slab = lax.axis_index("seq") * 8 + lax.axis_index("head")
    after, before = slab_peers()
    w_copy = pltpu.make_async_copy(conv_w, w_buf, w_sem)
    w_copy.start()
    count = greet(
        x_peers()
        + [zl_peer(), core_peer(), zh_peer(), after, before]
        + [peer for _, peer in y_peers()]
        + [peer for _, peer in group_peers()]
    )

    def flip(i, carry):
        cut = pl.ds(pl.multiple_of(i * 256, 256), 256)
        dkv_rows[i] = jnp.transpose(dkv[:, cut].astype(F32)).astype(BF16)
        return carry

    lax.fori_loop(0, 4, flip, 0, unroll=True)

    def query_weights(n, carry):
        cut = pl.ds(pl.multiple_of(n * 512, 512), 512)
        rows = x_all[:, :, :, cut].reshape(1024, 512)
        a1[0, :, :, cut] = nn(dqt[...], rows).astype(BF16).reshape(4, 48, 512)
        a1[1, :, :, cut] = gwo[:, cut].reshape(4, 48, 512)
        return carry

    lax.fori_loop(0, 3, query_weights, 0)
    met(count)
    links = Links(send, recv)
    early = Sum(links, a1, a2, a3, a4, a5, a6)
    late = Sum(links, b1, b2, b3, b4, b5, b6)
    early.swap()

    def terms_of(plane):
        def term(k, carry):
            i = plane * 2 + k
            t = nn(dq[i], w[0:DH]) + nn(dkv_rows[i], w[DH : 3 * DH])
            terms[pl.ds(2 * i, 2)] = t.astype(BF16).reshape(2, 128, C)
            return carry

        lax.fori_loop(0, 2, term, 0)

    scatter = Scatter(links, terms, s1, s2, s3, s4, s5, s6, s7)
    terms_of(1 - zl)
    scatter.begin_other()
    terms_of(zl)
    scatter.begin_own()
    early.over_y()

    def weights(n, carry):
        cut = pl.ds(pl.multiple_of(n * 512, 512), 512)
        rows = x_all[:, :, :, cut].reshape(1024, 512)
        b1[:, :, :, cut] = nn(dkv[...], rows).astype(BF16).reshape(2, 4, 48, 512)
        return carry

    lax.fori_loop(0, 3, weights, 0)
    late.swap()
    late.over_y()
    early.over_z()
    scatter.middle()
    late.over_z()
    early.spread()
    late.spread()
    scatter.end()
    out = exchange_out(links, s7, d_normed)
    mixed = exchange_out(links, mixed_in, mixed_out)
    early.mirror()
    late.mirror()
    for copy in out:
        copy.wait_recv()
    n_rows = skip[...].reshape(128, C).astype(F32) * rstd[...]
    g_rows = d_normed[...].reshape(128, C).astype(F32) * gain[...]
    mean = jnp.sum(g_rows * n_rows, axis=-1, keepdims=True) / C
    d_skip = grad[...].reshape(128, C).astype(F32) + rstd[...] * (g_rows - n_rows * mean)
    low, high = pl.ds(0, 128), pl.ds(128, 128)
    even = (slope[low] * d_skip).astype(BF16)
    odd = (slope[high] * d_skip).astype(BF16)
    for p, block in enumerate((even, odd)):
        rows = block.reshape(4, 32, C)
        edges[0, p], edges[1, p] = rows[:, 0], rows[:, 31]
    to_after = links.start(edges.at[1], halo.at[0], after)
    to_before = links.start(edges.at[0], halo.at[1], before)
    taps[2, low], taps[2, high] = even, odd
    taps[1, low], taps[3, high] = odd, even
    w_copy.wait()
    to_after.wait_recv()
    to_before.wait_recv()
    first, last = slab > 0, slab < 127
    even_before = shifted(even, halo[0, 0], False, first)
    odd_before = shifted(odd, halo[0, 1], False, first)
    even_after = shifted(even, halo[1, 0], True, last)
    odd_after = shifted(odd, halo[1, 1], True, last)
    taps[0, low], taps[0, high] = even_after, odd_after
    taps[1, high], taps[3, low] = even_after, odd_before
    taps[4, low], taps[4, high] = even_before, odd_before

    def conv_tile(n, carry):
        cut = pl.ds(pl.multiple_of(n * 256, 256), 256)
        v = nt(taps[0], w_buf[0, cut])
        for k in range(1, KW):
            v = v + nt(taps[k], w_buf[k, cut])
        grad_input[:, cut] = v.astype(BF16)
        return carry

    lax.fori_loop(0, 3, conv_tile, 0)
    early.end()
    late.end()
    gw_out[0:DH] = a6[0].reshape(DH, C)
    gwo_out[...] = a6[1].reshape(DH, C)
    gw_out[DH : 3 * DH] = b6[...].reshape(2 * DH, C)
    for copy in mixed:
        copy.wait_recv()
    links.finish()


def vmem_call(kernel, collective_id, inputs, outputs, scratch, limit, copies, hbm=0):
    spec = pl.BlockSpec(memory_space=VM)
    far = pl.BlockSpec(memory_space=pl.ANY)
    return pl.pallas_call(
        kernel,
        out_shape=[jax.ShapeDtypeStruct(shape, dtype) for shape, dtype in outputs],
        in_specs=[spec] * (len(inputs) - hbm) + [far] * hbm,
        out_specs=[spec] * len(outputs),
        scratch_shapes=[pltpu.SemaphoreType.DMA((copies,)), pltpu.SemaphoreType.DMA((copies,))] + scratch,
        compiler_params=pltpu.CompilerParams(
            collective_id=collective_id, has_side_effects=True, vmem_limit_bytes=limit << 20
        ),
    )(*inputs)


def body(enc_in, conv_weight, norm_gain, w_qkv, w_out, grad_out):
    enc = jnp.transpose(enc_in.reshape(32, 2, 4, 768), (1, 2, 0, 3))
    edges = jnp.stack([enc_in[:2], enc_in[62:]])
    grad = jnp.transpose(grad_out, (1, 0, 2))
    w = jnp.transpose(w_qkv, (0, 2, 1)).reshape(3 * DH, C)
    gain = norm_gain.reshape(1, C)
    skip, rstd, slope, x_all, g_own, q, qt, kvt = vmem_call(
        gather_kernel,
        0,
        [enc, edges, gain, grad, w, conv_weight],
        [
            ((4, 32, C), BF16),
            ((128, 1), F32),
            ((256, C), F32),
            ((8, 4, 32, C), BF16),
            ((4, 32, C), BF16),
            ((4, 256, DH), BF16),
            ((DH, 1024), BF16),
            ((2 * DH, 1024), BF16),
        ],
        [
            pltpu.SemaphoreType.DMA((6,)),
            VM((6, KW, 768, 256), BF16),
            VM((2, 2, 4, 768), BF16),
            VM((KW, 256, 768), BF16),
            VM((4, 32, C), BF16),
        ],
        45,
        40,
        1,
    )
    final, gwo, dq, dqt, dkv = vmem_call(
        attention_kernel,
        1,
        [g_own, q, qt, kvt, w_out],
        [
            ((4, 32, C), BF16),
            ((DH, C), BF16),
            ((4, 256, DH), BF16),
            ((DH, 1024), BF16),
            ((2 * DH, 1024), BF16),
        ],
        [
            VM((8, 4, 32, C), BF16),
            VM((4, 2 * DH, 1024), BF16),
            VM((4, 256, 1), F32),
            VM((4, 4, 256, 1), F32),
            VM((4, 256, 1), F32),
            VM((4, 256, DH), F32),
            VM((4, 4, 256, 1024), BF16),
            VM((4, 256, DH), BF16),
            VM((DH, 1024), BF16),
            VM((4, 256, DH), BF16),
            VM((DH, 1024), BF16),
            VM((4, 256, 1), F32),
            VM((4, 256, 1024), BF16),
            VM((4, 256, DH), F32),
            VM((2 * DH, 1024), F32),
            VM((3, 2 * DH, 1024), BF16),
            VM((3, 2 * DH, 1024), BF16),
            VM((8, 128, C), BF16),
        ]
        + SCATTER_SCRATCH[:-1],
        58,
        64,
    )
    mixed, gw, gwo, grad_input = vmem_call(
        gradient_kernel,
        2,
        [x_all, dq, dqt, dkv, w, gwo, final, skip, rstd, gain, slope, grad, conv_weight],
        [((4, 32, C), BF16), ((3 * DH, C), BF16), ((DH, C), BF16), ((256, 768), BF16)],
        [pltpu.SemaphoreType.DMA, VM((4, 256, 2 * DH), BF16), VM((8, 128, C), BF16)]
        + SCATTER_SCRATCH
        + SUM_SCRATCH * 2
        + [
            VM((KW, 768, C), BF16),
            VM((4, 32, C), BF16),
            VM((2, 2, 4, C), BF16),
            VM((2, 2, 4, C), BF16),
            VM((KW, 256, C), BF16),
        ],
        58,
        48,
        1,
    )
    mixed = (skip.astype(F32) + mixed.astype(F32)).astype(BF16)
    grad_input = jnp.transpose(grad_input.reshape(2, 4, 32, 768), (2, 0, 1, 3)).reshape(64, 4, 768)
    return (
        jnp.transpose(mixed, (1, 0, 2)),
        grad_input,
        jnp.transpose(gw.astype(F32).reshape(3, DH, C), (0, 2, 1)),
        gwo.astype(F32),
    )


def solution(mesh):
    return jax.shard_map(
        body,
        mesh=mesh,
        in_specs=(
            P(("seq", "head"), None, None),
            P(),
            P(),
            P(None, None, "head"),
            P("head", None),
            P(("seq", "head"), None, None),
        ),
        out_specs=(
            P(("seq", "head"), None, None),
            P(("seq", "head"), None, None),
            P(None, None, "head"),
            P("head", None),
        ),
        check_vma=False,
    )
```

```python
import math

import jax
import jax.numpy as jnp
from jax import lax
from jax.experimental import pallas as pl
from jax.experimental.pallas import tpu as pltpu
from jax.sharding import PartitionSpec as P

DH = 192
KW = 5
C = 1536
SCALE = DH ** (-0.5)
LOG2E = math.log2(math.e)
MESH = pl.DeviceIdType.MESH
F32 = jnp.float32
BF16 = jnp.bfloat16
VM = pltpu.VMEM


def coords():
    s = lax.axis_index("seq")
    h = lax.axis_index("head")
    return s // 4, (s // 2) % 2, s % 2, h // 4, h % 4


def device(y, zh, c, zl, x):
    return (y * 4 + zh * 2 + c, zl * 4 + x)


def x_peers():
    y, zh, c, zl, x = coords()
    return [device(y, zh, c, zl, (x + d) % 4) for d in (1, 2, 3)]


def zl_peer():
    y, zh, c, zl, x = coords()
    return device(y, zh, c, 1 - zl, x)


def core_peer():
    y, zh, c, zl, x = coords()
    return device(y, zh, 1 - c, zl, x)


def y_pair_peer():
    y, zh, c, zl, x = coords()
    return device(y + 1 - 2 * (y % 2), zh, c, zl, x)


def group():
    y, zh, c, zl, x = coords()
    return (y // 2) * 2 + zh


def group_peers():
    y, zh, c, zl, x = coords()
    peers = []
    for dy, dz in ((0, 1), (1, 0), (1, 1)):
        yh = (y // 2 + dy) % 2
        z2 = (zh + dz) % 2
        peers.append((yh * 2 + z2, device(yh * 2 + y % 2, z2, c, zl, x)))
    return peers


def greet(peers):
    sem = pltpu.get_barrier_semaphore()
    for peer in peers:
        pl.semaphore_signal(sem, inc=1, device_id=peer, device_id_type=MESH)
    return len(peers)


def met(count):
    pl.semaphore_wait(pltpu.get_barrier_semaphore(), count)


class Links:
    def __init__(self, send, recv):
        self.send, self.recv, self.used, self.all = send, recv, 0, []

    def start(self, src, dst, peer):
        copy = pltpu.make_async_remote_copy(
            src_ref=src,
            dst_ref=dst,
            send_sem=self.send.at[self.used],
            recv_sem=self.recv.at[self.used],
            device_id=peer,
            device_id_type=MESH,
        )
        self.used += 1
        self.all.append(copy)
        copy.start()
        return copy

    def finish(self):
        for copy in self.all:
            copy.wait_send()


def nt(a, b):
    return lax.dot_general(a, b, (((1,), (1,)), ((), ())), preferred_element_type=F32)


def nn(a, b):
    return lax.dot_general(a, b, (((1,), (0,)), ((), ())), preferred_element_type=F32)


def x_neighbours():
    y, zh, c, zl, x = coords()
    return device(y, zh, c, zl, (x + 1) % 4), device(y, zh, c, zl, (x + 3) % 4)


class Gather:
    def __init__(self, links, buf):
        self.links, self.buf = links, buf
        y, zh, c, zl, x = coords()
        self.zl, self.x = zl, x
        self.order = [group()] + [g for g, _ in group_peers()]

    def at(self, plane, dx, r):
        return self.buf.at[plane * 4 + (self.x + dx) % 4, self.order[r]]

    def begin(self, incoming):
        up, down = x_neighbours()
        start = self.links.start
        self.up, self.down, self.z = {}, {}, {}
        for r in range(4):
            if r > 0 and incoming is not None:
                incoming[r - 1].wait_recv()
            own = self.at(self.zl, 0, r)
            self.up[r] = start(own, own, up)
            self.down[r] = start(own, own, down)
            self.z[r] = start(own, own, zl_peer())

    def forward(self):
        up, down = x_neighbours()
        z, zl, other = zl_peer(), self.zl, 1 - self.zl

        def send(part, peer):
            return self.links.start(part, part, peer)

        self.up[0].wait_recv()
        self.relay_0 = send(self.at(zl, 3, 0), up)
        self.low_0 = send(self.at(zl, 3, 0), z)
        self.down[1].wait_recv()
        self.relay_1 = send(self.at(zl, 1, 1), down)
        self.high_1 = send(self.at(zl, 1, 1), z)
        self.z[2].wait_recv()
        self.low_2 = send(self.at(other, 0, 2), up)
        self.high_2 = send(self.at(other, 0, 2), down)
        self.z[3].wait_recv()
        self.high_3 = send(self.at(other, 0, 3), down)
        self.low_3 = send(self.at(other, 0, 3), up)
        self.down[0].wait_recv()
        self.high_0 = send(self.at(zl, 1, 0), z)
        self.up[1].wait_recv()
        self.low_1 = send(self.at(zl, 3, 1), z)
        self.up[2].wait_recv()
        self.relay_2 = send(self.at(zl, 3, 2), up)
        self.down[3].wait_recv()
        self.relay_3 = send(self.at(zl, 1, 3), down)

    def relay(self):
        up, down = x_neighbours()
        z, zl, other = zl_peer(), self.zl, 1 - self.zl

        def send(part, peer):
            return self.links.start(part, part, peer)

        self.relay_0.wait_recv()
        self.far_0 = send(self.at(zl, 2, 0), z)
        self.relay_1.wait_recv()
        self.far_1 = send(self.at(zl, 2, 1), z)
        self.low_2.wait_recv()
        self.far_2 = send(self.at(other, 3, 2), up)
        self.high_3.wait_recv()
        self.far_3 = send(self.at(other, 1, 3), down)

    def steps(self):
        other = 1 - self.zl
        return [
            (self.zl, 3, [self.up[3]]),
            (self.zl, 1, [self.down[2]]),
            (other, 0, [self.z[0], self.z[1]]),
            (self.zl, 2, [self.relay_2, self.relay_3]),
            (other, 3, [self.low_0, self.low_1, self.low_3]),
            (other, 1, [self.high_0, self.high_1, self.high_2]),
            (other, 2, [self.far_0, self.far_1, self.far_2, self.far_3]),
        ]

    def end(self):
        for _, _, copies in self.steps():
            for copy in copies:
                copy.wait_recv()


def exchange_in(links, slab, buf, me):
    mine = group()
    buf[me, mine] = slab[mine]
    return [links.start(slab.at[g], buf.at[me, mine], peer) for g, peer in group_peers()]


class Scatter:
    def __init__(self, links, terms, first, second, last, pair, pair_sum, third, final):
        self.links, self.terms = links, terms
        self.first, self.second, self.last = first, second, last
        self.pair, self.pair_sum, self.third, self.final = pair, pair_sum, third, final
        y, zh, c, zl, x = coords()
        self.zl, self.x = zl, x
        self.me = zl * 4 + x

    def begin_other(self):
        zl, x, links = self.zl, self.x, self.links
        other = 1 - zl
        low, high = pl.ds(0, 64), pl.ds(64, 64)
        self.c_pair = [
            links.start(self.terms.at[other * 4 + k, high], self.pair.at[k], zl_peer()) for k in range(4)
        ]
        self.c_second = [
            links.start(self.terms.at[other * 4 + (x + d) % 4, low], self.second.at[d - 1], peer)
            for d, peer in zip((1, 2, 3), x_peers())
        ]

    def begin_own(self):
        zl, x, links = self.zl, self.x, self.links
        low = pl.ds(0, 64)
        self.c_first = [
            links.start(self.terms.at[zl * 4 + (x + d) % 4, low], self.first.at[d - 1], peer)
            for d, peer in zip((1, 2, 3), x_peers())
        ]

    def middle(self):
        zl, x, links = self.zl, self.x, self.links
        low, high = pl.ds(0, 64), pl.ds(64, 64)
        for copy in self.c_pair:
            copy.wait_recv()

        def add_pair(k, carry):
            self.pair_sum[k] = (
                self.terms[zl * 4 + k, high].astype(F32) + self.pair[k].astype(F32)
            ).astype(BF16)
            return carry

        lax.fori_loop(0, 4, add_pair, 0)
        self.c_third = [
            links.start(self.pair_sum.at[(x + d) % 4], self.third.at[d - 1], peer)
            for d, peer in zip((1, 2, 3), x_peers())
        ]
        for copy in self.c_second:
            copy.wait_recv()
        total = self.terms[(1 - zl) * 4 + x, low].astype(F32)
        for k in range(3):
            total = total + self.second[k].astype(F32)
        self.second[3] = total.astype(BF16)
        self.c_last = links.start(self.second.at[3], self.last, zl_peer())

    def end(self):
        zl, x = self.zl, self.x
        low = pl.ds(0, 64)
        for copy in self.c_first + self.c_third + [self.c_last]:
            copy.wait_recv()
        total = self.terms[self.me, low].astype(F32) + self.last[...].astype(F32)
        for k in range(3):
            total = total + self.first[k].astype(F32)
        self.final[0:2] = total.astype(BF16).reshape(2, 32, C)
        total = self.pair_sum[x].astype(F32)
        for k in range(3):
            total = total + self.third[k].astype(F32)
        self.final[2:4] = total.astype(BF16).reshape(2, 32, C)


SCATTER_SCRATCH = [
    VM((3, 64, C), BF16),
    VM((4, 64, C), BF16),
    VM((64, C), BF16),
    VM((4, 64, C), BF16),
    VM((4, 64, C), BF16),
    VM((3, 64, C), BF16),
    VM((4, 32, C), BF16),
]


def exchange_out(links, final, out):
    mine = group()
    out[mine] = final[mine]
    return [links.start(final.at[g], out.at[mine], peer) for g, peer in group_peers()]


def rows_of(ref, i):
    return ref[pl.ds(2 * i, 2)].reshape(256, C)


def slab_peers():
    me = lax.axis_index("seq") * 8 + lax.axis_index("head")
    after, before = (me + 1) % 128, (me + 127) % 128
    return (after // 8, after % 8), (before // 8, before % 8)


def shifted(block, edge, up, here):
    width = block.shape[-1]
    wide = block.astype(F32)
    place = lax.broadcasted_iota(jnp.int32, (128, width), 0) % 32
    fill = jnp.where(here, edge.astype(F32), 0.0)
    fill = jnp.concatenate([jnp.broadcast_to(fill[b : b + 1], (32, width)) for b in range(4)], axis=0)
    if up:
        return jnp.where(place == 31, fill, pltpu.roll(wide, 127, 0)).astype(BF16)
    return jnp.where(place == 0, fill, pltpu.roll(wide, 1, 0)).astype(BF16)


def attention_kernel(
    enc, edges, gain, grad, w, w_out, conv_w,
    skip, rstd, slope, x_all, mixed_out, gwo, dq_out, dqt_out, dkv_out,
    send, recv, w_sem, w_buf, halo, taps, normed,
    g_all, q, qt, kv, peak, chunk_peak, total, o_acc, e_all, ob, ot, do, dot_, delta,
    ds, dq_acc, acc, dkv_send, dkv_recv, terms, s1, s2, s3, s4, s5, s6,
):
    y, zh, c, zl, x = coords()
    me = zl * 4 + x
    slab = lax.axis_index("seq") * 8 + lax.axis_index("head")
    after, before = slab_peers()

    def tile_copy(n):
        cut = pl.ds(pl.multiple_of(n * 256, 256), 256)
        return pltpu.make_async_copy(conv_w.at[:, :, cut], w_buf.at[n % 3], w_sem.at[n % 3])

    for n in range(3):
        tile_copy(n).start()
    met(
        greet(
            x_peers()
            + [zl_peer(), core_peer(), y_pair_peer(), after, before]
            + [peer for _, peer in group_peers()]
        )
    )
    links = Links(send, recv)
    to_after = links.start(edges.at[1], halo.at[0], after)
    to_before = links.start(edges.at[0], halo.at[1], before)
    grad_copies = exchange_in(links, grad, g_all, me)
    even, odd = enc[0].reshape(128, 768), enc[1].reshape(128, 768)
    low, high = pl.ds(0, 128), pl.ds(128, 128)
    taps[2, low], taps[2, high] = even, odd
    taps[3, low], taps[1, high] = odd, even
    to_after.wait_recv()
    to_before.wait_recv()
    first, last = slab > 0, slab < 127
    even_before = shifted(even, halo[0, 0], False, first)
    odd_before = shifted(odd, halo[0, 1], False, first)
    even_after = shifted(even, halo[1, 0], True, last)
    odd_after = shifted(odd, halo[1, 1], True, last)
    taps[0, low], taps[0, high] = even_before, odd_before
    taps[1, low], taps[3, high] = odd_before, even_after
    taps[4, low], taps[4, high] = even_after, odd_after
    root = math.sqrt(2.0 / math.pi)

    def conv_tile(n, squares):
        tile_copy(n).wait()
        cut = pl.ds(pl.multiple_of(n * 256, 256), 256)
        v = nn(taps[0], w_buf[n % 3, 0])
        for k in range(1, KW):
            v = v + nn(taps[k], w_buf[n % 3, k])

        @pl.when(n < 3)
        def _():
            tile_copy(n + 3).start()

        v2 = v * v
        t = jnp.tanh(root * v * (1.0 + 0.044715 * v2))
        half = 0.5 * (1.0 + t)
        act = v * half
        pull = half + 0.5 * v * (1.0 - t * t) * (root * (1.0 + 3.0 * 0.044715 * v2))
        slope[:, cut] = pull * 0.5
        s = ((act[0:128] + act[128:256]) * 0.5).astype(BF16)
        skip[:, :, cut] = s.reshape(4, 32, 256)
        s = s.astype(F32)
        return squares + jnp.sum(s * s, axis=-1, keepdims=True)

    squares = lax.fori_loop(0, 6, conv_tile, jnp.zeros((128, 1), F32))
    r = lax.rsqrt(squares / C + 1e-06)
    rstd[...] = r
    value = skip[...].reshape(128, C).astype(F32) * r * gain[...]
    normed[...] = value.astype(BF16).reshape(4, 32, C)
    copies = exchange_in(links, normed, x_all, me)
    gather = Gather(links, x_all)
    gather.begin(copies)
    kv_core, kv_pair = [], []

    def project(k):
        rows = x_all[k].reshape(128, C)
        part = nt(rows, w[0:DH])
        q[k // 2, pl.ds((k % 2) * 128, 128)] = part.astype(BF16)
        cut = pl.ds(pl.multiple_of(k * 128, 128), 128)
        qt[:, cut] = jnp.transpose(part).astype(BF16)
        kv[0, :, cut] = nt(w[DH : 3 * DH], rows).astype(BF16)
        kv_pair.append((cut, links.start(kv.at[0, :, cut], kv.at[2, :, cut], y_pair_peer())))
        kv_core.append(links.start(kv.at[0, :, cut], kv.at[1, :, cut], core_peer()))

    project(me)
    gather.forward()
    for copy in grad_copies:
        copy.wait_recv()
    late = Gather(links, g_all)
    late.begin(None)
    gather.up[3].wait_recv()
    project(zl * 4 + (x + 3) % 4)
    gather.relay()
    for n, (plane, dx, waits) in enumerate(gather.steps()):
        if n > 0:
            for copy in waits:
                copy.wait_recv()
            project(plane * 4 + (x + dx) % 4)
    kv_relay = []

    def pass_on(first, last):
        for cut, copy in kv_pair[first:last]:
            copy.wait_recv()
            kv_relay.append(links.start(kv.at[2, :, cut], kv.at[3, :, cut], core_peer()))

    pass_on(0, 6)
    peak[...] = jnp.full_like(peak, -jnp.inf)
    total[...] = jnp.zeros_like(total)
    o_acc[...] = jnp.zeros_like(o_acc)
    unit = SCALE * LOG2E

    def forward(j):
        def tile(i, carry):
            s = nn(q[i], kv[j, 0:DH])
            old = peak[i]
            new = jnp.maximum(old, jnp.max(s, axis=-1, keepdims=True))
            peak[i] = new
            chunk_peak[j, i] = new
            fade = jnp.exp2((old - new) * unit)
            e = jnp.exp2(s * unit - new * unit)
            total[i] = total[i] * fade + jnp.sum(e, axis=-1, keepdims=True)
            eb = e.astype(BF16)
            e_all[j, i] = eb
            o_acc[i] = o_acc[i] * fade + nt(eb, kv[j, DH : 2 * DH])
            return carry

        lax.fori_loop(0, 4, tile, 0, unroll=True)

    forward(0)
    pass_on(6, 8)
    for copy in kv_core:
        copy.wait_recv()
    late.forward()
    forward(1)
    late.relay()
    forward(2)
    for copy in kv_relay:
        copy.wait_recv()
    forward(3)

    def finish_tile(i, carry):
        inverse = 1.0 / total[i]
        o = o_acc[i] * inverse
        o_acc[i] = o
        ob[i] = o.astype(BF16)
        ot[:, pl.ds(pl.multiple_of(i * 256, 256), 256)] = jnp.transpose(o).astype(BF16)
        for j in range(4):
            chunk_peak[j, i] = jnp.exp2((chunk_peak[j, i] - peak[i]) * unit) * inverse
        term = nn(ob[i], w_out[...]).astype(BF16)
        terms[pl.ds(2 * i, 2)] = term.reshape(2, 128, C)
        return carry

    lax.fori_loop(0, 4, finish_tile, 0)
    scatter = Scatter(links, terms, s1, s2, s3, s4, s5, s6, mixed_out)
    late.end()
    scatter.begin_other()
    scatter.begin_own()

    def output_gradient(i, carry):
        d = nt(rows_of(g_all, i), w_out[...])
        db = d.astype(BF16)
        do[i] = db
        db = db.astype(F32)
        dot_[:, pl.ds(pl.multiple_of(i * 256, 256), 256)] = jnp.transpose(db).astype(BF16)
        delta[i] = jnp.sum(db * o_acc[i], axis=-1, keepdims=True)
        dq_acc[i] = jnp.zeros((256, DH), F32)
        return carry

    lax.fori_loop(0, 4, output_gradient, 0)

    def backward(j):
        def tile(i, carry):
            p = e_all[j, i].astype(F32) * chunk_peak[j, i]
            e_all[j, i] = p.astype(BF16)
            dp = nn(do[i], kv[j, DH : 2 * DH])
            d = (p * (dp - delta[i])).astype(BF16)
            ds[i] = d
            dq_acc[i] += nt(d, kv[j, 0:DH])
            return carry

        lax.fori_loop(0, 4, tile, 0, unroll=True)

        def columns(n, carry):
            cut = pl.ds(pl.multiple_of(n * 256, 256), 256)
            acc[0:DH, cut] = nn(qt[...], ds[:, :, cut].reshape(1024, 256)) * SCALE
            acc[DH : 2 * DH, cut] = nn(dot_[...], e_all[j, :, :, cut].reshape(1024, 256))
            return carry

        lax.fori_loop(0, 4, columns, 0)

    backward(3)
    dkv_send[0] = acc[...].astype(BF16)
    far = links.start(dkv_send.at[0], dkv_recv.at[0], core_peer())
    backward(2)
    far.wait_recv()
    dkv_send[1] = (acc[...] + dkv_recv[0].astype(F32)).astype(BF16)
    pair = links.start(dkv_send.at[1], dkv_recv.at[1], y_pair_peer())
    backward(1)
    dkv_send[2] = acc[...].astype(BF16)
    near = links.start(dkv_send.at[2], dkv_recv.at[2], core_peer())
    scatter.middle()
    backward(0)

    def query(i, carry):
        d = dq_acc[i] * SCALE
        dq_out[i] = d.astype(BF16)
        dqt_out[:, pl.ds(pl.multiple_of(i * 256, 256), 256)] = jnp.transpose(d).astype(BF16)
        return carry

    lax.fori_loop(0, 4, query, 0)

    def w_out_gradient(n, carry):
        cut = pl.ds(pl.multiple_of(n * 512, 512), 512)
        gwo[:, cut] = nn(ot[...], g_all[:, :, :, cut].reshape(1024, 512)).astype(BF16)
        return carry

    lax.fori_loop(0, 3, w_out_gradient, 0)
    scatter.end()
    near.wait_recv()
    pair.wait_recv()
    dkv_out[...] = (acc[...] + dkv_recv[1].astype(F32) + dkv_recv[2].astype(F32)).astype(BF16)
    links.finish()


def y_peers():
    y, zh, c, zl, x = coords()
    return [((y + d) % 4, device((y + d) % 4, zh, c, zl, x)) for d in (1, 2, 3)]


def zh_peer():
    y, zh, c, zl, x = coords()
    return device(y, 1 - zh, c, zl, x)


class Sum:
    def __init__(self, links, part, half_in, half, y_in, z_in, done):
        self.links, self.part, self.half_in, self.half = links, part, half_in, half
        self.y_in, self.z_in, self.done = y_in, z_in, done
        self.y, zh, self.c, zl, x = coords()

    def swap(self):
        self.c_swap = self.links.start(self.part.at[1 - self.c], self.half_in, core_peer())

    def over_y(self):
        self.c_swap.wait_recv()

        def add(k, carry):
            self.half[k] = (self.part[self.c, k].astype(F32) + self.half_in[k].astype(F32)).astype(BF16)
            return carry

        lax.fori_loop(0, 4, add, 0)
        self.c_y = [
            self.links.start(self.half.at[k], self.y_in.at[n], peer) for n, (k, peer) in enumerate(y_peers())
        ]

    def over_z(self):
        for copy in self.c_y:
            copy.wait_recv()
        total = self.half[self.y].astype(F32)
        for n in range(3):
            total = total + self.y_in[n].astype(F32)
        self.z_in[0] = total.astype(BF16)
        self.c_z = self.links.start(self.z_in.at[0], self.z_in.at[1], zh_peer())

    def spread(self):
        self.c_z.wait_recv()
        total = self.z_in[0].astype(F32) + self.z_in[1].astype(F32)
        self.done[self.c, self.y] = total.astype(BF16)
        piece = self.done.at[self.c, self.y]
        self.c_spread = [self.links.start(piece, piece, peer) for _, peer in y_peers()]

    def mirror(self):
        for copy in self.c_spread:
            copy.wait_recv()
        rows = self.done.at[self.c]
        self.c_mirror = self.links.start(rows, rows, core_peer())

    def end(self):
        self.c_mirror.wait_recv()


SUM_SCRATCH = [
    VM((2, 4, 48, C), BF16),
    VM((4, 48, C), BF16),
    VM((4, 48, C), BF16),
    VM((3, 48, C), BF16),
    VM((2, 48, C), BF16),
    VM((2, 4, 48, C), BF16),
]


def gradient_kernel(
    x_all, dq, dqt, dkv, w, gwo, mixed_in, skip, rstd, gain, slope, grad, conv_w,
    mixed_out, gw_out, gwo_out, grad_input,
    send, recv, w_sem, dkv_rows, terms, s1, s2, s3, s4, s5, s6, s7,
    a1, a2, a3, a4, a5, a6, b1, b2, b3, b4, b5, b6, w_buf, d_normed, edges, halo, taps,
):
    y, zh, c, zl, x = coords()
    slab = lax.axis_index("seq") * 8 + lax.axis_index("head")
    after, before = slab_peers()
    w_copy = pltpu.make_async_copy(conv_w, w_buf, w_sem)
    w_copy.start()
    count = greet(
        x_peers()
        + [zl_peer(), core_peer(), zh_peer(), after, before]
        + [peer for _, peer in y_peers()]
        + [peer for _, peer in group_peers()]
    )

    def flip(i, carry):
        cut = pl.ds(pl.multiple_of(i * 256, 256), 256)
        dkv_rows[i] = jnp.transpose(dkv[:, cut].astype(F32)).astype(BF16)
        return carry

    lax.fori_loop(0, 4, flip, 0, unroll=True)

    def query_weights(n, carry):
        cut = pl.ds(pl.multiple_of(n * 512, 512), 512)
        rows = x_all[:, :, :, cut].reshape(1024, 512)
        a1[0, :, :, cut] = nn(dqt[...], rows).astype(BF16).reshape(4, 48, 512)
        a1[1, :, :, cut] = gwo[:, cut].reshape(4, 48, 512)
        return carry

    lax.fori_loop(0, 3, query_weights, 0)
    met(count)
    links = Links(send, recv)
    early = Sum(links, a1, a2, a3, a4, a5, a6)
    late = Sum(links, b1, b2, b3, b4, b5, b6)
    early.swap()

    def terms_of(plane):
        def term(k, carry):
            i = plane * 2 + k
            t = nn(dq[i], w[0:DH]) + nn(dkv_rows[i], w[DH : 3 * DH])
            terms[pl.ds(2 * i, 2)] = t.astype(BF16).reshape(2, 128, C)
            return carry

        lax.fori_loop(0, 2, term, 0)

    scatter = Scatter(links, terms, s1, s2, s3, s4, s5, s6, s7)
    terms_of(1 - zl)
    scatter.begin_other()
    terms_of(zl)
    scatter.begin_own()
    early.over_y()

    def weights(n, carry):
        cut = pl.ds(pl.multiple_of(n * 512, 512), 512)
        rows = x_all[:, :, :, cut].reshape(1024, 512)
        b1[:, :, :, cut] = nn(dkv[...], rows).astype(BF16).reshape(2, 4, 48, 512)
        return carry

    lax.fori_loop(0, 3, weights, 0)
    late.swap()
    late.over_y()
    early.over_z()
    scatter.middle()
    late.over_z()
    early.spread()
    late.spread()
    scatter.end()
    out = exchange_out(links, s7, d_normed)
    mixed = exchange_out(links, mixed_in, mixed_out)
    early.mirror()
    late.mirror()
    for copy in out:
        copy.wait_recv()
    n_rows = skip[...].reshape(128, C).astype(F32) * rstd[...]
    g_rows = d_normed[...].reshape(128, C).astype(F32) * gain[...]
    mean = jnp.sum(g_rows * n_rows, axis=-1, keepdims=True) / C
    d_skip = grad[...].reshape(128, C).astype(F32) + rstd[...] * (g_rows - n_rows * mean)
    low, high = pl.ds(0, 128), pl.ds(128, 128)
    even = (slope[low] * d_skip).astype(BF16)
    odd = (slope[high] * d_skip).astype(BF16)
    for p, block in enumerate((even, odd)):
        rows = block.reshape(4, 32, C)
        edges[0, p], edges[1, p] = rows[:, 0], rows[:, 31]
    to_after = links.start(edges.at[1], halo.at[0], after)
    to_before = links.start(edges.at[0], halo.at[1], before)
    taps[2, low], taps[2, high] = even, odd
    taps[1, low], taps[3, high] = odd, even
    w_copy.wait()
    to_after.wait_recv()
    to_before.wait_recv()
    first, last = slab > 0, slab < 127
    even_before = shifted(even, halo[0, 0], False, first)
    odd_before = shifted(odd, halo[0, 1], False, first)
    even_after = shifted(even, halo[1, 0], True, last)
    odd_after = shifted(odd, halo[1, 1], True, last)
    taps[0, low], taps[0, high] = even_after, odd_after
    taps[1, high], taps[3, low] = even_after, odd_before
    taps[4, low], taps[4, high] = even_before, odd_before

    def conv_tile(n, carry):
        cut = pl.ds(pl.multiple_of(n * 256, 256), 256)
        v = nt(taps[0], w_buf[0, cut])
        for k in range(1, KW):
            v = v + nt(taps[k], w_buf[k, cut])
        grad_input[:, cut] = v.astype(BF16)
        return carry

    lax.fori_loop(0, 3, conv_tile, 0)
    early.end()
    late.end()
    gw_out[0:DH] = a6[0].reshape(DH, C)
    gwo_out[...] = a6[1].reshape(DH, C)
    gw_out[DH : 3 * DH] = b6[...].reshape(2 * DH, C)
    for copy in mixed:
        copy.wait_recv()
    links.finish()


def vmem_call(kernel, collective_id, inputs, outputs, scratch, limit, copies, hbm=0):
    spec = pl.BlockSpec(memory_space=VM)
    far = pl.BlockSpec(memory_space=pl.ANY)
    return pl.pallas_call(
        kernel,
        out_shape=[jax.ShapeDtypeStruct(shape, dtype) for shape, dtype in outputs],
        in_specs=[spec] * (len(inputs) - hbm) + [far] * hbm,
        out_specs=[spec] * len(outputs),
        scratch_shapes=[pltpu.SemaphoreType.DMA((copies,)), pltpu.SemaphoreType.DMA((copies,))] + scratch,
        compiler_params=pltpu.CompilerParams(
            collective_id=collective_id, has_side_effects=True, vmem_limit_bytes=limit << 20
        ),
    )(*inputs)


def body(enc_in, conv_weight, norm_gain, w_qkv, w_out, grad_out):
    enc = jnp.transpose(enc_in.reshape(32, 2, 4, 768), (1, 2, 0, 3))
    edges = jnp.stack([enc_in[:2], enc_in[62:]])
    grad = jnp.transpose(grad_out, (1, 0, 2))
    w = jnp.transpose(w_qkv, (0, 2, 1)).reshape(3 * DH, C)
    gain = norm_gain.reshape(1, C)
    skip, rstd, slope, x_all, final, gwo, dq, dqt, dkv = vmem_call(
        attention_kernel,
        0,
        [enc, edges, gain, grad, w, w_out, conv_weight],
        [
            ((4, 32, C), BF16),
            ((128, 1), F32),
            ((256, C), F32),
            ((8, 4, 32, C), BF16),
            ((4, 32, C), BF16),
            ((DH, C), BF16),
            ((4, 256, DH), BF16),
            ((DH, 1024), BF16),
            ((2 * DH, 1024), BF16),
        ],
        [
            pltpu.SemaphoreType.DMA((3,)),
            VM((3, KW, 768, 256), BF16),
            VM((2, 2, 4, 768), BF16),
            VM((KW, 256, 768), BF16),
            VM((4, 32, C), BF16),
            VM((8, 4, 32, C), BF16),
            VM((4, 256, DH), BF16),
            VM((DH, 1024), BF16),
            VM((4, 2 * DH, 1024), BF16),
            VM((4, 256, 1), F32),
            VM((4, 4, 256, 1), F32),
            VM((4, 256, 1), F32),
            VM((4, 256, DH), F32),
            VM((4, 4, 256, 1024), BF16),
            VM((4, 256, DH), BF16),
            VM((DH, 1024), BF16),
            VM((4, 256, DH), BF16),
            VM((DH, 1024), BF16),
            VM((4, 256, 1), F32),
            VM((4, 256, 1024), BF16),
            VM((4, 256, DH), F32),
            VM((2 * DH, 1024), F32),
            VM((3, 2 * DH, 1024), BF16),
            VM((3, 2 * DH, 1024), BF16),
            VM((8, 128, C), BF16),
        ]
        + SCATTER_SCRATCH[:-1],
        61,
        120,
        1,
    )
    mixed, gw, gwo, grad_input = vmem_call(
        gradient_kernel,
        1,
        [x_all, dq, dqt, dkv, w, gwo, final, skip, rstd, gain, slope, grad, conv_weight],
        [((4, 32, C), BF16), ((3 * DH, C), BF16), ((DH, C), BF16), ((256, 768), BF16)],
        [pltpu.SemaphoreType.DMA, VM((4, 256, 2 * DH), BF16), VM((8, 128, C), BF16)]
        + SCATTER_SCRATCH
        + SUM_SCRATCH * 2
        + [
            VM((KW, 768, C), BF16),
            VM((4, 32, C), BF16),
            VM((2, 2, 4, C), BF16),
            VM((2, 2, 4, C), BF16),
            VM((KW, 256, C), BF16),
        ],
        58,
        48,
        1,
    )
    mixed = (skip.astype(F32) + mixed.astype(F32)).astype(BF16)
    grad_input = jnp.transpose(grad_input.reshape(2, 4, 32, 768), (2, 0, 1, 3)).reshape(64, 4, 768)
    return (
        jnp.transpose(mixed, (1, 0, 2)),
        grad_input,
        jnp.transpose(gw.astype(F32).reshape(3, DH, C), (0, 2, 1)),
        gwo.astype(F32),
    )


def solution(mesh):
    return jax.shard_map(
        body,
        mesh=mesh,
        in_specs=(
            P(("seq", "head"), None, None),
            P(),
            P(),
            P(None, None, "head"),
            P("head", None),
            P(("seq", "head"), None, None),
        ),
        out_specs=(
            P(("seq", "head"), None, None),
            P(("seq", "head"), None, None),
            P(None, None, "head"),
            P("head", None),
        ),
        check_vma=False,
    )
```

```python
import math

import jax
import jax.numpy as jnp
from jax import lax
from jax.experimental import pallas as pl
from jax.experimental.pallas import tpu as pltpu
from jax.sharding import PartitionSpec as P

DH = 192
KW = 5
C = 1536
SCALE = DH ** (-0.5)
LOG2E = math.log2(math.e)
MESH = pl.DeviceIdType.MESH
F32 = jnp.float32
BF16 = jnp.bfloat16
VM = pltpu.VMEM


def coords():
    s = lax.axis_index("seq")
    h = lax.axis_index("head")
    return s // 4, (s // 2) % 2, s % 2, h // 4, h % 4


def device(y, zh, c, zl, x):
    return (y * 4 + zh * 2 + c, zl * 4 + x)


def x_peers():
    y, zh, c, zl, x = coords()
    return [device(y, zh, c, zl, (x + d) % 4) for d in (1, 2, 3)]


def zl_peer():
    y, zh, c, zl, x = coords()
    return device(y, zh, c, 1 - zl, x)


def core_peer():
    y, zh, c, zl, x = coords()
    return device(y, zh, 1 - c, zl, x)


def y_pair_peer():
    y, zh, c, zl, x = coords()
    return device(y + 1 - 2 * (y % 2), zh, c, zl, x)


def group():
    y, zh, c, zl, x = coords()
    return (y // 2) * 2 + zh


def group_peers():
    y, zh, c, zl, x = coords()
    peers = []
    for dy, dz in ((0, 1), (1, 0), (1, 1)):
        yh = (y // 2 + dy) % 2
        z2 = (zh + dz) % 2
        peers.append((yh * 2 + z2, device(yh * 2 + y % 2, z2, c, zl, x)))
    return peers


def greet(peers):
    sem = pltpu.get_barrier_semaphore()
    for peer in peers:
        pl.semaphore_signal(sem, inc=1, device_id=peer, device_id_type=MESH)
    return len(peers)


def met(count):
    pl.semaphore_wait(pltpu.get_barrier_semaphore(), count)


class Links:
    def __init__(self, send, recv):
        self.send, self.recv, self.used, self.all = send, recv, 0, []

    def start(self, src, dst, peer):
        copy = pltpu.make_async_remote_copy(
            src_ref=src,
            dst_ref=dst,
            send_sem=self.send.at[self.used],
            recv_sem=self.recv.at[self.used],
            device_id=peer,
            device_id_type=MESH,
        )
        self.used += 1
        self.all.append(copy)
        copy.start()
        return copy

    def finish(self):
        for copy in self.all:
            copy.wait_send()


def nt(a, b):
    return lax.dot_general(a, b, (((1,), (1,)), ((), ())), preferred_element_type=F32)


def nn(a, b):
    return lax.dot_general(a, b, (((1,), (0,)), ((), ())), preferred_element_type=F32)


def x_neighbours():
    y, zh, c, zl, x = coords()
    return device(y, zh, c, zl, (x + 1) % 4), device(y, zh, c, zl, (x + 3) % 4)


class Gather:
    def __init__(self, links, buf):
        self.links, self.buf = links, buf
        y, zh, c, zl, x = coords()
        self.zl, self.x = zl, x
        self.order = [group()] + [g for g, _ in group_peers()]

    def at(self, plane, dx, r):
        return self.buf.at[plane * 4 + (self.x + dx) % 4, self.order[r]]

    def begin(self, incoming):
        up, down = x_neighbours()
        start = self.links.start
        self.up, self.down, self.z = {}, {}, {}
        for r in range(4):
            if r > 0 and incoming is not None:
                incoming[r - 1].wait_recv()
            own = self.at(self.zl, 0, r)
            self.up[r] = start(own, own, up)
            self.down[r] = start(own, own, down)
            self.z[r] = start(own, own, zl_peer())

    def forward(self):
        up, down = x_neighbours()
        z, zl, other = zl_peer(), self.zl, 1 - self.zl

        def send(part, peer):
            return self.links.start(part, part, peer)

        self.up[0].wait_recv()
        self.relay_0 = send(self.at(zl, 3, 0), up)
        self.low_0 = send(self.at(zl, 3, 0), z)
        self.down[1].wait_recv()
        self.relay_1 = send(self.at(zl, 1, 1), down)
        self.high_1 = send(self.at(zl, 1, 1), z)
        self.z[2].wait_recv()
        self.low_2 = send(self.at(other, 0, 2), up)
        self.high_2 = send(self.at(other, 0, 2), down)
        self.z[3].wait_recv()
        self.high_3 = send(self.at(other, 0, 3), down)
        self.low_3 = send(self.at(other, 0, 3), up)
        self.down[0].wait_recv()
        self.high_0 = send(self.at(zl, 1, 0), z)
        self.up[1].wait_recv()
        self.low_1 = send(self.at(zl, 3, 1), z)
        self.up[2].wait_recv()
        self.relay_2 = send(self.at(zl, 3, 2), up)
        self.down[3].wait_recv()
        self.relay_3 = send(self.at(zl, 1, 3), down)

    def relay(self):
        up, down = x_neighbours()
        z, zl, other = zl_peer(), self.zl, 1 - self.zl

        def send(part, peer):
            return self.links.start(part, part, peer)

        self.relay_0.wait_recv()
        self.far_0 = send(self.at(zl, 2, 0), z)
        self.relay_1.wait_recv()
        self.far_1 = send(self.at(zl, 2, 1), z)
        self.low_2.wait_recv()
        self.far_2 = send(self.at(other, 3, 2), up)
        self.high_3.wait_recv()
        self.far_3 = send(self.at(other, 1, 3), down)

    def steps(self):
        other = 1 - self.zl
        return [
            (self.zl, 3, [self.up[3]]),
            (self.zl, 1, [self.down[2]]),
            (other, 0, [self.z[0], self.z[1]]),
            (self.zl, 2, [self.relay_2, self.relay_3]),
            (other, 3, [self.low_0, self.low_1, self.low_3]),
            (other, 1, [self.high_0, self.high_1, self.high_2]),
            (other, 2, [self.far_0, self.far_1, self.far_2, self.far_3]),
        ]

    def end(self):
        for _, _, copies in self.steps():
            for copy in copies:
                copy.wait_recv()


def exchange_in(links, slab, buf, me):
    mine = group()
    buf[me, mine] = slab[mine]
    return [links.start(slab.at[g], buf.at[me, mine], peer) for g, peer in group_peers()]


class Scatter:
    def __init__(self, links, terms, first, second, last, pair, pair_sum, third, final):
        self.links, self.terms = links, terms
        self.first, self.second, self.last = first, second, last
        self.pair, self.pair_sum, self.third, self.final = pair, pair_sum, third, final
        y, zh, c, zl, x = coords()
        self.zl, self.x = zl, x
        self.me = zl * 4 + x
        self.other_half, self.own_half = 1 - y // 2, y // 2
        self.low = pl.ds(pl.multiple_of(self.other_half * 64, 64), 64)
        self.high = pl.ds(pl.multiple_of(self.own_half * 64, 64), 64)

    def begin_other(self):
        zl, x, links = self.zl, self.x, self.links
        other = 1 - zl
        low, high = self.low, self.high
        self.c_pair = [
            links.start(self.terms.at[other * 4 + k, high], self.pair.at[k], zl_peer()) for k in range(4)
        ]
        self.c_second = [
            links.start(self.terms.at[other * 4 + (x + d) % 4, low], self.second.at[d - 1], peer)
            for d, peer in zip((1, 2, 3), x_peers())
        ]

    def begin_own(self):
        zl, x, links = self.zl, self.x, self.links
        low = self.low
        self.c_first = [
            links.start(self.terms.at[zl * 4 + (x + d) % 4, low], self.first.at[d - 1], peer)
            for d, peer in zip((1, 2, 3), x_peers())
        ]

    def middle(self):
        zl, x, links = self.zl, self.x, self.links
        low, high = self.low, self.high
        for copy in self.c_pair:
            copy.wait_recv()

        def add_pair(k, carry):
            self.pair_sum[k] = (
                self.terms[zl * 4 + k, high].astype(F32) + self.pair[k].astype(F32)
            ).astype(BF16)
            return carry

        lax.fori_loop(0, 4, add_pair, 0)
        self.c_third = [
            links.start(self.pair_sum.at[(x + d) % 4], self.third.at[d - 1], peer)
            for d, peer in zip((1, 2, 3), x_peers())
        ]
        for copy in self.c_second:
            copy.wait_recv()
        total = self.terms[(1 - zl) * 4 + x, low].astype(F32)
        for k in range(3):
            total = total + self.second[k].astype(F32)
        self.second[3] = total.astype(BF16)
        self.c_last = links.start(self.second.at[3], self.last, zl_peer())

    def end_low(self):
        for copy in self.c_first + [self.c_last]:
            copy.wait_recv()
        total = self.terms[self.me, self.low].astype(F32) + self.last[...].astype(F32)
        for k in range(3):
            total = total + self.first[k].astype(F32)
        self.final[pl.ds(self.other_half * 2, 2)] = total.astype(BF16).reshape(2, 32, C)

    def end_high(self):
        for copy in self.c_third:
            copy.wait_recv()
        total = self.pair_sum[self.x].astype(F32)
        for k in range(3):
            total = total + self.third[k].astype(F32)
        self.final[pl.ds(self.own_half * 2, 2)] = total.astype(BF16).reshape(2, 32, C)


SCATTER_SCRATCH = [
    VM((3, 64, C), BF16),
    VM((4, 64, C), BF16),
    VM((64, C), BF16),
    VM((4, 64, C), BF16),
    VM((4, 64, C), BF16),
    VM((3, 64, C), BF16),
    VM((4, 32, C), BF16),
]


def exchange_out(links, final, out):
    mine = group()
    out[mine] = final[mine]
    return [links.start(final.at[g], out.at[mine], peer) for g, peer in group_peers()]


def rows_of(ref, i):
    return ref[pl.ds(2 * i, 2)].reshape(256, C)


def slab_peers():
    me = lax.axis_index("seq") * 8 + lax.axis_index("head")
    after, before = (me + 1) % 128, (me + 127) % 128
    return (after // 8, after % 8), (before // 8, before % 8)


def shifted(block, edge, up, here):
    width = block.shape[-1]
    wide = block.astype(F32)
    place = lax.broadcasted_iota(jnp.int32, (128, width), 0) % 32
    fill = jnp.where(here, edge.astype(F32), 0.0)
    fill = jnp.concatenate([jnp.broadcast_to(fill[b : b + 1], (32, width)) for b in range(4)], axis=0)
    if up:
        return jnp.where(place == 31, fill, pltpu.roll(wide, 127, 0)).astype(BF16)
    return jnp.where(place == 0, fill, pltpu.roll(wide, 1, 0)).astype(BF16)


def attention_kernel(
    enc, edges, gain, grad, w, w_out, conv_w,
    skip, rstd, slope, x_all, mixed_out, gwo, dq_out, dqt_out, dkv_out,
    send, recv, w_sem, w_buf, halo, taps, normed,
    g_all, q, qt, kv, peak, chunk_peak, total, o_acc, e_all, ob, ot, do, dot_, delta,
    ds, dq_acc, acc, dkv_send, dkv_recv, terms, s1, s2, s3, s4, s5, s6,
):
    y, zh, c, zl, x = coords()
    me = zl * 4 + x
    slab = lax.axis_index("seq") * 8 + lax.axis_index("head")
    after, before = slab_peers()

    def tile_copy(n):
        cut = pl.ds(pl.multiple_of(n * 256, 256), 256)
        return pltpu.make_async_copy(conv_w.at[:, :, cut], w_buf.at[n % 3], w_sem.at[n % 3])

    for n in range(3):
        tile_copy(n).start()
    met(
        greet(
            x_peers()
            + [zl_peer(), core_peer(), y_pair_peer(), after, before]
            + [peer for _, peer in group_peers()]
        )
    )
    links = Links(send, recv)
    to_after = links.start(edges.at[1], halo.at[0], after)
    to_before = links.start(edges.at[0], halo.at[1], before)
    grad_copies = exchange_in(links, grad, g_all, me)
    even, odd = enc[0].reshape(128, 768), enc[1].reshape(128, 768)
    low, high = pl.ds(0, 128), pl.ds(128, 128)
    taps[2, low], taps[2, high] = even, odd
    taps[3, low], taps[1, high] = odd, even
    to_after.wait_recv()
    to_before.wait_recv()
    first, last = slab > 0, slab < 127
    even_before = shifted(even, halo[0, 0], False, first)
    odd_before = shifted(odd, halo[0, 1], False, first)
    even_after = shifted(even, halo[1, 0], True, last)
    odd_after = shifted(odd, halo[1, 1], True, last)
    taps[0, low], taps[0, high] = even_before, odd_before
    taps[1, low], taps[3, high] = odd_before, even_after
    taps[4, low], taps[4, high] = even_after, odd_after
    root = math.sqrt(2.0 / math.pi)

    def conv_tile(n, squares):
        tile_copy(n).wait()
        cut = pl.ds(pl.multiple_of(n * 256, 256), 256)
        v = nn(taps[0], w_buf[n % 3, 0])
        for k in range(1, KW):
            v = v + nn(taps[k], w_buf[n % 3, k])

        @pl.when(n < 3)
        def _():
            tile_copy(n + 3).start()

        v2 = v * v
        t = jnp.tanh(root * v * (1.0 + 0.044715 * v2))
        half = 0.5 * (1.0 + t)
        act = v * half
        pull = half + 0.5 * v * (1.0 - t * t) * (root * (1.0 + 3.0 * 0.044715 * v2))
        slope[:, cut] = pull * 0.5
        s = ((act[0:128] + act[128:256]) * 0.5).astype(BF16)
        skip[:, :, cut] = s.reshape(4, 32, 256)
        s = s.astype(F32)
        return squares + jnp.sum(s * s, axis=-1, keepdims=True)

    squares = lax.fori_loop(0, 6, conv_tile, jnp.zeros((128, 1), F32))
    r = lax.rsqrt(squares / C + 1e-06)
    rstd[...] = r
    value = skip[...].reshape(128, C).astype(F32) * r * gain[...]
    normed[...] = value.astype(BF16).reshape(4, 32, C)
    copies = exchange_in(links, normed, x_all, me)
    gather = Gather(links, x_all)
    gather.begin(copies)
    kv_core, kv_pair = [], []

    def project(k):
        rows = x_all[k].reshape(128, C)
        part = nt(rows, w[0:DH])
        q[k // 2, pl.ds((k % 2) * 128, 128)] = part.astype(BF16)
        cut = pl.ds(pl.multiple_of(k * 128, 128), 128)
        qt[:, cut] = jnp.transpose(part).astype(BF16)
        kv[0, :, cut] = nt(w[DH : 3 * DH], rows).astype(BF16)
        kv_pair.append((cut, links.start(kv.at[0, :, cut], kv.at[2, :, cut], y_pair_peer())))
        kv_core.append(links.start(kv.at[0, :, cut], kv.at[1, :, cut], core_peer()))

    project(me)
    gather.forward()
    for copy in grad_copies:
        copy.wait_recv()
    late = Gather(links, g_all)
    late.begin(None)
    gather.up[3].wait_recv()
    project(zl * 4 + (x + 3) % 4)
    gather.relay()
    for n, (plane, dx, waits) in enumerate(gather.steps()):
        if n > 0:
            for copy in waits:
                copy.wait_recv()
            project(plane * 4 + (x + dx) % 4)
    kv_relay = []

    def pass_on(first, last):
        for cut, copy in kv_pair[first:last]:
            copy.wait_recv()
            kv_relay.append(links.start(kv.at[2, :, cut], kv.at[3, :, cut], core_peer()))

    pass_on(0, 6)
    peak[...] = jnp.full_like(peak, -jnp.inf)
    total[...] = jnp.zeros_like(total)
    o_acc[...] = jnp.zeros_like(o_acc)
    unit = SCALE * LOG2E

    def forward(j):
        def tile(i, carry):
            s = nn(q[i], kv[j, 0:DH])
            old = peak[i]
            new = jnp.maximum(old, jnp.max(s, axis=-1, keepdims=True))
            peak[i] = new
            chunk_peak[j, i] = new
            fade = jnp.exp2((old - new) * unit)
            e = jnp.exp2(s * unit - new * unit)
            total[i] = total[i] * fade + jnp.sum(e, axis=-1, keepdims=True)
            eb = e.astype(BF16)
            e_all[j, i] = eb
            o_acc[i] = o_acc[i] * fade + nt(eb, kv[j, DH : 2 * DH])
            return carry

        lax.fori_loop(0, 4, tile, 0, unroll=True)

    forward(0)
    pass_on(6, 8)
    for copy in kv_core:
        copy.wait_recv()
    late.forward()
    forward(1)
    late.relay()
    forward(2)
    for copy in kv_relay:
        copy.wait_recv()
    forward(3)

    def finish_tile(i, carry):
        inverse = 1.0 / total[i]
        o = o_acc[i] * inverse
        o_acc[i] = o
        ob[i] = o.astype(BF16)
        ot[:, pl.ds(pl.multiple_of(i * 256, 256), 256)] = jnp.transpose(o).astype(BF16)
        for j in range(4):
            chunk_peak[j, i] = jnp.exp2((chunk_peak[j, i] - peak[i]) * unit) * inverse
        term = nn(ob[i], w_out[...]).astype(BF16)
        terms[pl.ds(2 * i, 2)] = term.reshape(2, 128, C)
        return carry

    lax.fori_loop(0, 4, finish_tile, 0)
    scatter = Scatter(links, terms, s1, s2, s3, s4, s5, s6, mixed_out)
    late.end()
    scatter.begin_other()
    scatter.begin_own()

    def output_gradient(i, carry):
        d = nt(rows_of(g_all, i), w_out[...])
        db = d.astype(BF16)
        do[i] = db
        db = db.astype(F32)
        dot_[:, pl.ds(pl.multiple_of(i * 256, 256), 256)] = jnp.transpose(db).astype(BF16)
        delta[i] = jnp.sum(db * o_acc[i], axis=-1, keepdims=True)
        dq_acc[i] = jnp.zeros((256, DH), F32)
        return carry

    lax.fori_loop(0, 4, output_gradient, 0)

    def backward(j):
        def tile(i, carry):
            p = e_all[j, i].astype(F32) * chunk_peak[j, i]
            e_all[j, i] = p.astype(BF16)
            dp = nn(do[i], kv[j, DH : 2 * DH])
            d = (p * (dp - delta[i])).astype(BF16)
            ds[i] = d
            dq_acc[i] += nt(d, kv[j, 0:DH])
            return carry

        lax.fori_loop(0, 4, tile, 0, unroll=True)

        def columns(n, carry):
            cut = pl.ds(pl.multiple_of(n * 256, 256), 256)
            acc[0:DH, cut] = nn(qt[...], ds[:, :, cut].reshape(1024, 256)) * SCALE
            acc[DH : 2 * DH, cut] = nn(dot_[...], e_all[j, :, :, cut].reshape(1024, 256))
            return carry

        lax.fori_loop(0, 4, columns, 0)

    backward(3)
    dkv_send[0] = acc[...].astype(BF16)
    far = links.start(dkv_send.at[0], dkv_recv.at[0], core_peer())
    backward(2)
    far.wait_recv()
    dkv_send[1] = (acc[...] + dkv_recv[0].astype(F32)).astype(BF16)
    pair = links.start(dkv_send.at[1], dkv_recv.at[1], y_pair_peer())
    backward(1)
    dkv_send[2] = acc[...].astype(BF16)
    near = links.start(dkv_send.at[2], dkv_recv.at[2], core_peer())
    scatter.middle()
    backward(0)

    def query(i, carry):
        d = dq_acc[i] * SCALE
        dq_out[i] = d.astype(BF16)
        dqt_out[:, pl.ds(pl.multiple_of(i * 256, 256), 256)] = jnp.transpose(d).astype(BF16)
        return carry

    lax.fori_loop(0, 4, query, 0)

    def w_out_gradient(n, carry):
        cut = pl.ds(pl.multiple_of(n * 512, 512), 512)
        gwo[:, cut] = nn(ot[...], g_all[:, :, :, cut].reshape(1024, 512)).astype(BF16)
        return carry

    lax.fori_loop(0, 3, w_out_gradient, 0)
    scatter.end_low()
    scatter.end_high()
    near.wait_recv()
    pair.wait_recv()
    dkv_out[...] = (acc[...] + dkv_recv[1].astype(F32) + dkv_recv[2].astype(F32)).astype(BF16)
    links.finish()


def y_peers():
    y, zh, c, zl, x = coords()
    return [((y + d) % 4, device((y + d) % 4, zh, c, zl, x)) for d in (1, 2, 3)]


def zh_peer():
    y, zh, c, zl, x = coords()
    return device(y, 1 - zh, c, zl, x)


class Sum:
    def __init__(self, links, part, half_in, half, y_in, z_in, done):
        self.links, self.part, self.half_in, self.half = links, part, half_in, half
        self.y_in, self.z_in, self.done = y_in, z_in, done
        self.y, zh, self.c, zl, x = coords()

    def swap(self):
        self.c_swap = self.links.start(self.part.at[1 - self.c], self.half_in, core_peer())

    def over_y(self):
        self.c_swap.wait_recv()

        def add(k, carry):
            self.half[k] = (self.part[self.c, k].astype(F32) + self.half_in[k].astype(F32)).astype(BF16)
            return carry

        lax.fori_loop(0, 4, add, 0)
        self.c_y = [
            self.links.start(self.half.at[k], self.y_in.at[n], peer) for n, (k, peer) in enumerate(y_peers())
        ]

    def over_z(self):
        for copy in self.c_y:
            copy.wait_recv()
        total = self.half[self.y].astype(F32)
        for n in range(3):
            total = total + self.y_in[n].astype(F32)
        self.z_in[0] = total.astype(BF16)
        self.c_z = self.links.start(self.z_in.at[0], self.z_in.at[1], zh_peer())

    def spread(self):
        self.c_z.wait_recv()
        total = self.z_in[0].astype(F32) + self.z_in[1].astype(F32)
        self.done[self.c, self.y] = total.astype(BF16)
        piece = self.done.at[self.c, self.y]
        self.c_spread = [self.links.start(piece, piece, peer) for _, peer in y_peers()]

    def mirror(self):
        for copy in self.c_spread:
            copy.wait_recv()
        rows = self.done.at[self.c]
        self.c_mirror = self.links.start(rows, rows, core_peer())

    def end(self):
        self.c_mirror.wait_recv()


SUM_SCRATCH = [
    VM((2, 4, 48, C), BF16),
    VM((4, 48, C), BF16),
    VM((4, 48, C), BF16),
    VM((3, 48, C), BF16),
    VM((2, 48, C), BF16),
    VM((2, 4, 48, C), BF16),
]


def gradient_kernel(
    x_all, dq, dqt, dkv, w, gwo, mixed_in, skip, rstd, gain, slope, grad, conv_w,
    mixed_out, gw_out, gwo_out, grad_input,
    send, recv, w_sem, dkv_rows, terms, s1, s2, s3, s4, s5, s6, s7,
    a1, a2, a3, a4, a5, a6, b1, b2, b3, b4, b5, b6, w_buf, d_normed, edges, halo, taps,
):
    y, zh, c, zl, x = coords()
    slab = lax.axis_index("seq") * 8 + lax.axis_index("head")
    after, before = slab_peers()
    w_copy = pltpu.make_async_copy(conv_w, w_buf, w_sem)
    w_copy.start()
    count = greet(
        x_peers()
        + [zl_peer(), core_peer(), zh_peer(), after, before]
        + [peer for _, peer in y_peers()]
        + [peer for _, peer in group_peers()]
    )

    def flip(i, carry):
        cut = pl.ds(pl.multiple_of(i * 256, 256), 256)
        dkv_rows[i] = jnp.transpose(dkv[:, cut].astype(F32)).astype(BF16)
        return carry

    lax.fori_loop(0, 4, flip, 0, unroll=True)

    def query_weights(n, carry):
        cut = pl.ds(pl.multiple_of(n * 512, 512), 512)
        rows = x_all[:, :, :, cut].reshape(1024, 512)
        a1[0, :, :, cut] = nn(dqt[...], rows).astype(BF16).reshape(4, 48, 512)
        a1[1, :, :, cut] = gwo[:, cut].reshape(4, 48, 512)
        return carry

    lax.fori_loop(0, 3, query_weights, 0)
    met(count)
    links = Links(send, recv)
    early = Sum(links, a1, a2, a3, a4, a5, a6)
    late = Sum(links, b1, b2, b3, b4, b5, b6)
    early.swap()

    def terms_of(plane):
        def term(k, carry):
            i = plane * 2 + k
            t = nn(dq[i], w[0:DH]) + nn(dkv_rows[i], w[DH : 3 * DH])
            terms[pl.ds(2 * i, 2)] = t.astype(BF16).reshape(2, 128, C)
            return carry

        lax.fori_loop(0, 2, term, 0)

    scatter = Scatter(links, terms, s1, s2, s3, s4, s5, s6, s7)
    terms_of(1 - zl)
    scatter.begin_other()
    terms_of(zl)
    scatter.begin_own()
    early.over_y()

    def weights(n, carry):
        cut = pl.ds(pl.multiple_of(n * 512, 512), 512)
        rows = x_all[:, :, :, cut].reshape(1024, 512)
        b1[:, :, :, cut] = nn(dkv[...], rows).astype(BF16).reshape(2, 4, 48, 512)
        return carry

    lax.fori_loop(0, 3, weights, 0)
    late.swap()
    late.over_y()
    early.over_z()
    scatter.middle()
    early.spread()
    mine = group()
    scatter.end_low()
    near, *others = group_peers()
    out = [links.start(s7.at[g], d_normed.at[mine], peer) for g, peer in others]
    late.over_z()
    scatter.end_high()
    out.append(links.start(s7.at[near[0]], d_normed.at[mine], near[1]))
    d_normed[mine] = s7[mine]
    late.spread()
    early.mirror()
    for copy in out:
        copy.wait_recv()
    mixed = exchange_out(links, mixed_in, mixed_out)
    n_rows = skip[...].reshape(128, C).astype(F32) * rstd[...]
    g_rows = d_normed[...].reshape(128, C).astype(F32) * gain[...]
    mean = jnp.sum(g_rows * n_rows, axis=-1, keepdims=True) / C
    d_skip = grad[...].reshape(128, C).astype(F32) + rstd[...] * (g_rows - n_rows * mean)
    low, high = pl.ds(0, 128), pl.ds(128, 128)
    even = (slope[low] * d_skip).astype(BF16)
    odd = (slope[high] * d_skip).astype(BF16)
    for p, block in enumerate((even, odd)):
        rows = block.reshape(4, 32, C)
        edges[0, p], edges[1, p] = rows[:, 0], rows[:, 31]
    to_after = links.start(edges.at[1], halo.at[0], after)
    to_before = links.start(edges.at[0], halo.at[1], before)
    late.mirror()
    taps[2, low], taps[2, high] = even, odd
    taps[1, low], taps[3, high] = odd, even
    w_copy.wait()
    to_after.wait_recv()
    to_before.wait_recv()
    first, last = slab > 0, slab < 127
    even_before = shifted(even, halo[0, 0], False, first)
    odd_before = shifted(odd, halo[0, 1], False, first)
    even_after = shifted(even, halo[1, 0], True, last)
    odd_after = shifted(odd, halo[1, 1], True, last)
    taps[0, low], taps[0, high] = even_after, odd_after
    taps[1, high], taps[3, low] = even_after, odd_before
    taps[4, low], taps[4, high] = even_before, odd_before

    def conv_tile(n, carry):
        cut = pl.ds(pl.multiple_of(n * 256, 256), 256)
        v = nt(taps[0], w_buf[0, cut])
        for k in range(1, KW):
            v = v + nt(taps[k], w_buf[k, cut])
        grad_input[:, cut] = v.astype(BF16)
        return carry

    lax.fori_loop(0, 3, conv_tile, 0)
    early.end()
    late.end()
    gw_out[0:DH] = a6[0].reshape(DH, C)
    gwo_out[...] = a6[1].reshape(DH, C)
    gw_out[DH : 3 * DH] = b6[...].reshape(2 * DH, C)
    for copy in mixed:
        copy.wait_recv()
    links.finish()


def vmem_call(kernel, collective_id, inputs, outputs, scratch, limit, copies, hbm=0):
    spec = pl.BlockSpec(memory_space=VM)
    far = pl.BlockSpec(memory_space=pl.ANY)
    return pl.pallas_call(
        kernel,
        out_shape=[jax.ShapeDtypeStruct(shape, dtype) for shape, dtype in outputs],
        in_specs=[spec] * (len(inputs) - hbm) + [far] * hbm,
        out_specs=[spec] * len(outputs),
        scratch_shapes=[pltpu.SemaphoreType.DMA((copies,)), pltpu.SemaphoreType.DMA((copies,))] + scratch,
        compiler_params=pltpu.CompilerParams(
            collective_id=collective_id, has_side_effects=True, vmem_limit_bytes=limit << 20
        ),
    )(*inputs)


def body(enc_in, conv_weight, norm_gain, w_qkv, w_out, grad_out):
    enc = jnp.transpose(enc_in.reshape(32, 2, 4, 768), (1, 2, 0, 3))
    edges = jnp.stack([enc_in[:2], enc_in[62:]])
    grad = jnp.transpose(grad_out, (1, 0, 2))
    w = jnp.transpose(w_qkv, (0, 2, 1)).reshape(3 * DH, C)
    gain = norm_gain.reshape(1, C)
    skip, rstd, slope, x_all, final, gwo, dq, dqt, dkv = vmem_call(
        attention_kernel,
        0,
        [enc, edges, gain, grad, w, w_out, conv_weight],
        [
            ((4, 32, C), BF16),
            ((128, 1), F32),
            ((256, C), F32),
            ((8, 4, 32, C), BF16),
            ((4, 32, C), BF16),
            ((DH, C), BF16),
            ((4, 256, DH), BF16),
            ((DH, 1024), BF16),
            ((2 * DH, 1024), BF16),
        ],
        [
            pltpu.SemaphoreType.DMA((3,)),
            VM((3, KW, 768, 256), BF16),
            VM((2, 2, 4, 768), BF16),
            VM((KW, 256, 768), BF16),
            VM((4, 32, C), BF16),
            VM((8, 4, 32, C), BF16),
            VM((4, 256, DH), BF16),
            VM((DH, 1024), BF16),
            VM((4, 2 * DH, 1024), BF16),
            VM((4, 256, 1), F32),
            VM((4, 4, 256, 1), F32),
            VM((4, 256, 1), F32),
            VM((4, 256, DH), F32),
            VM((4, 4, 256, 1024), BF16),
            VM((4, 256, DH), BF16),
            VM((DH, 1024), BF16),
            VM((4, 256, DH), BF16),
            VM((DH, 1024), BF16),
            VM((4, 256, 1), F32),
            VM((4, 256, 1024), BF16),
            VM((4, 256, DH), F32),
            VM((2 * DH, 1024), F32),
            VM((3, 2 * DH, 1024), BF16),
            VM((3, 2 * DH, 1024), BF16),
            VM((8, 128, C), BF16),
        ]
        + SCATTER_SCRATCH[:-1],
        61,
        120,
        1,
    )
    mixed, gw, gwo, grad_input = vmem_call(
        gradient_kernel,
        1,
        [x_all, dq, dqt, dkv, w, gwo, final, skip, rstd, gain, slope, grad, conv_weight],
        [((4, 32, C), BF16), ((3 * DH, C), BF16), ((DH, C), BF16), ((256, 768), BF16)],
        [pltpu.SemaphoreType.DMA, VM((4, 256, 2 * DH), BF16), VM((8, 128, C), BF16)]
        + SCATTER_SCRATCH
        + SUM_SCRATCH * 2
        + [
            VM((KW, 768, C), BF16),
            VM((4, 32, C), BF16),
            VM((2, 2, 4, C), BF16),
            VM((2, 2, 4, C), BF16),
            VM((KW, 256, C), BF16),
        ],
        58,
        48,
        1,
    )
    mixed = (skip.astype(F32) + mixed.astype(F32)).astype(BF16)
    grad_input = jnp.transpose(grad_input.reshape(2, 4, 32, 768), (2, 0, 1, 3)).reshape(64, 4, 768)
    return (
        jnp.transpose(mixed, (1, 0, 2)),
        grad_input,
        jnp.transpose(gw.astype(F32).reshape(3, DH, C), (0, 2, 1)),
        gwo.astype(F32),
    )


def solution(mesh):
    return jax.shard_map(
        body,
        mesh=mesh,
        in_specs=(
            P(("seq", "head"), None, None),
            P(),
            P(),
            P(None, None, "head"),
            P("head", None),
            P(("seq", "head"), None, None),
        ),
        out_specs=(
            P(("seq", "head"), None, None),
            P(("seq", "head"), None, None),
            P(None, None, "head"),
            P("head", None),
        ),
        check_vma=False,
    )
```
